256 devices in a mesh: expert: 32 (over y, x, core), narrow: 8 (over z).
Axes of the slice: x: 4, y: 4, z: 8, core: 2. Of those that a mesh axis runs over, the one named last changes fastest.
Arguments:
- feats: bfloat16 [262144, 512], P(('expert', 'narrow')), may hold values from -6 to 6
- cotangent: bfloat16 [262144, 512], P(('expert', 'narrow')), may hold values from -0.59765625 to 0.59765625
- routes: int32 [262144, 1], P(('expert', 'narrow')), may hold values from 0 to 31; in each aligned block of 1024 rows (0 to 1023, 1024 to 2047, ...) at most 64 rows name the same one
- image_ids: int32 [262144], P(('expert', 'narrow')), may hold values from 0 to 2047, as said below
- codes: bfloat16 [2048, 48], replicated, may hold values from -6 to 6
- params: bfloat16 [32, 2096, 512], P('expert', 'narrow'), may hold values from -0.375 to 0.375
Outputs:
- out_rows: bfloat16 [262144, 512], P(('expert', 'narrow'))
- feat_grad: bfloat16 [262144, 512], P(('expert', 'narrow'))
- param_grad: float32 [32, 2096, 512], P('expert', 'narrow')
- code_grad: float32 [2048, 48], P(('expert', 'narrow'))
The draws below stay inside these ranges and needn't reach their ends.
Inputs may be any that keep to these rules, and one draw needn't show every extreme that they name: `routes`: among the rows of one device no expert is named more than 64 times, and on some device some expert is named exactly 64 times. `image_ids`: the rows of the device with flat index f over expert+narrow (expert index slowest) name only images f * 8 to f * 8 + 2 * 8 - 1, taken modulo 2048.
All inputs are finite; a program needn't handle non-finite values.
Results may differ from the reference program's by a relative error of at most 0.017.
Values may be sent and summed in bfloat16 or wider, within the bound.
No kernel may reach another device: no remote copies, remote signals or barrier semaphores. Data moves between devices by JAX's collectives and lax.ppermute only.
A program may use at most 128 MiB of HBM per device.

```python
import math
import jax
import jax.numpy as jnp
import numpy as np
from jax import lax

D = 512
CODE = 48
LAYERS = 4
ROWS_DEV = 1024
IMG_DEV = 8
EXPERTS = 32
CAP = 64
PROWS = 2096
ROWS = 262144
IMAGES = 2048
N_EXPERT = 32
N_NARROW = 8


def draw_image_ids(key, part):
    row_numbers = jnp.arange(ROWS, dtype=jnp.int32)
    device_no = row_numbers // ROWS_DEV
    jitter = jax.random.randint(key, (ROWS,), 0, 2 * IMG_DEV, dtype=jnp.int32)
    return (device_no * IMG_DEV + jitter) % IMAGES


def block_scale(stream_key, extent, shards, low, top_value):
    gain, own = 1.0, jax.random.fold_in(stream_key, 6)
    for dim, blocks in shards:
        heights = jnp.exp(jax.random.uniform(jax.random.fold_in(own, dim), (blocks,), jnp.float32, low / len(shards), top_value / len(shards)))
        gain = gain * jnp.repeat(heights, extent[dim] // blocks).reshape([-1 if axis == dim else 1 for axis in range(len(extent))])
    return gain


def assign_block(own_key, own, number, rows, number_of, top, most, lean):
    ranking = jax.random.permutation(own_key, number_of)
    crowded, common = portions_of(number_of, rows * top, most, lean, True), portions_of(number_of, rows * top, most, lean, False)
    places = jnp.arange(number_of)

    def named(sizes, offset_by):
        used = int((sizes > 0).sum())
        fixed = max(1, used // 4)
        shifted = fixed + (places - fixed + offset_by * (used - fixed)) % max(1, number_of - fixed)
        return jnp.zeros((number_of,), jnp.int32).at[ranking[jnp.where(places < fixed, places, shifted)]].set(jnp.asarray(sizes, jnp.int32))

    sizes = jnp.where(number % 4 == 0, named(crowded, number // 4), named(common, number - number // 4 - 1))
    mixed = jax.random.permutation(jax.random.fold_in(own, 3), number_of)
    source_of, receiver = mixed[0:number_of // 2 * 2:2], mixed[1:number_of // 2 * 2:2]
    slack = jnp.minimum(sizes[source_of] - 1, most - sizes[receiver]) // 2
    slack = jnp.where((source_of == ranking[0]) | (receiver == ranking[0]) | (sizes[receiver] == 0), 0, jnp.maximum(slack, 0))
    shifted = jax.random.randint(jax.random.fold_in(own, 4), (number_of // 2,), 0, 1 << 20) % (slack + 1)
    sizes = sizes.at[source_of].add(-shifted).at[receiver].add(shifted)
    members = jnp.searchsorted(jnp.cumsum(sizes), jnp.arange(rows * top), side="right").astype(jnp.int32)
    table = members.reshape(top, rows).T
    table = table[jax.random.permutation(jax.random.fold_in(own, 1), rows)]
    offset_by = jax.random.randint(jax.random.fold_in(own, 2), (rows, 1), 0, top)
    return jnp.take_along_axis(table, (jnp.arange(top)[None, :] + offset_by) % top, axis=1)


def portions_of(count, total, most, slope, full):
    loads = [(1 << 20) // math.isqrt(standing ** slope) + 1 for standing in range(1, count + 1)]
    largest = most if full else min(most, max(-(-total // count), total * loads[0] // sum(loads)))
    least = 1 if total - largest >= count - 1 else 0
    given, spare = [largest] + [least] * (count - 1), total - largest - least * (count - 1)
    while spare > 0:
        movable = [i for i in range(1, count) if given[i] < largest] or [i for i in range(1, count) if given[i] < most]
        whole, left = sum([loads[i] for i in movable]), spare
        for i in movable:
            addition = min(most - given[i], max(1, left * loads[i] // whole), spare)
            given[i] = given[i] + addition
            spare = spare - addition
    return np.array(given)


def scatter_about(own_key, dims, deviation, bound, cuts=(), held_as=jnp.bfloat16):
    factor_of = block_scale(own_key, dims, cuts, -0.22, 0.18) if cuts else 1.0
    entries = jax.random.normal(own_key, dims, jnp.float32) * deviation * factor_of
    return jnp.minimum(jnp.maximum(entries, -bound), bound).astype(held_as)


def setup_inputs(seed: int = 0) -> dict:
    arg_keys = jax.random.split(jax.random.key(seed), 7)
    feats = scatter_about(arg_keys[0], (ROWS, D), 1.0, 6.0, ((0, 256),))
    cotangent = scatter_about(arg_keys[1], (ROWS, D), 0.1, 0.59765625, ((0, 256),))
    routes_keys = jax.random.split(jax.random.fold_in(arg_keys[2], 1), ROWS // ROWS_DEV)
    routes_turns = jax.random.permutation(jax.random.fold_in(arg_keys[2], 3), ROWS // ROWS_DEV)
    routes = jax.vmap(lambda own, number: assign_block(jax.random.fold_in(arg_keys[2], 2), own, number, ROWS_DEV, EXPERTS, 1, CAP, 2))(routes_keys, routes_turns).reshape((ROWS, 1))
    image_ids = draw_image_ids(jax.random.fold_in(arg_keys[6], 71), 0)
    codes = scatter_about(arg_keys[4], (IMAGES, CODE), 1.0, 6.0)
    params = scatter_about(arg_keys[5], (EXPERTS, PROWS, D), (D // 2) ** -0.5, 0.375, ((0, 32), (1, 8)))
    return {"feats": feats, "cotangent": cotangent, "routes": routes, "image_ids": image_ids, "codes": codes, "params": params}


def forward(weights, row_block, code_rows, depth_count):
    feature_width = row_block.shape[1]
    code_matrix = weights[depth_count * feature_width:]
    current = row_block
    inputs = []
    preacts = []
    for layer_no in range(depth_count):
        inputs.append(current)
        layer_weights = weights[layer_no * feature_width:(layer_no + 1) * feature_width]
        preact = jnp.dot(current, layer_weights, preferred_element_type=jnp.float32)
        if layer_no == 0:
            preact = preact + jnp.dot(code_rows, code_matrix, preferred_element_type=jnp.float32)
        preacts.append(preact)
        current = jax.nn.silu(preact).astype(jnp.bfloat16)
    inputs.append(code_rows)
    return current, tuple(inputs), tuple(preacts)


def backward(weights, preacts, cotangent, depth_count):
    feature_width = cotangent.shape[1]
    code_matrix = weights[depth_count * feature_width:]
    upstream = cotangent.astype(jnp.float32)
    errors = []
    for layer_no in range(depth_count - 1, -1, -1):
        preact = preacts[layer_no]
        sigmoid_value = jax.nn.sigmoid(preact)
        error_rows = (upstream * sigmoid_value * (1.0 + preact * (1.0 - sigmoid_value))).astype(jnp.bfloat16)
        errors.insert(0, error_rows)
        layer_weights = weights[layer_no * feature_width:(layer_no + 1) * feature_width]
        upstream = jnp.dot(error_rows, layer_weights.T, preferred_element_type=jnp.float32)
    code_back = jnp.dot(errors[0], code_matrix.T, preferred_element_type=jnp.float32).astype(jnp.bfloat16)
    return upstream.astype(jnp.bfloat16), code_back, tuple(errors)


def param_terms(inputs, errors):
    depth_count = len(errors)
    blocks = []
    for layer_no in range(depth_count):
        blocks.append(jnp.dot(inputs[layer_no].T, errors[layer_no], preferred_element_type=jnp.float32))
    blocks.append(jnp.dot(inputs[depth_count].T, errors[0], preferred_element_type=jnp.float32))
    return jnp.concatenate(blocks, axis=0)


def reference(feats, cotangent, routes, image_ids, codes, params):
    devices = N_EXPERT * N_NARROW
    experts = params.shape[0]
    targets = routes[:, 0].reshape(devices, ROWS_DEV)
    onehot = (targets[:, :, None] == jnp.arange(experts, dtype=jnp.int32)[None, None, :]).astype(jnp.int32)
    slot_ids = jnp.sum(jnp.cumsum(onehot, axis=1) * onehot, axis=2) - 1
    positions = jnp.arange(devices, dtype=jnp.int32)[:, None] * CAP + slot_ids
    row_numbers = jnp.arange(ROWS, dtype=jnp.int32).reshape(devices, ROWS_DEV)
    slot_table = jnp.full((experts, devices * CAP), ROWS, jnp.int32).at[targets, positions].set(row_numbers)
    code_rows = codes[image_ids]

    def per_expert(state_now, pieces):
        out_all, feat_all, code_all = state_now
        weights, picked = pieces
        safe_ids = jnp.minimum(picked, ROWS - 1)
        live_mask = (picked < ROWS)[:, None]
        chosen_rows = jnp.where(live_mask, feats[safe_ids], jnp.zeros_like(feats[safe_ids]))
        chosen_codes = jnp.where(live_mask, code_rows[safe_ids], jnp.zeros_like(code_rows[safe_ids]))
        chosen_cot = jnp.where(live_mask, cotangent[safe_ids], jnp.zeros_like(cotangent[safe_ids]))
        outcome, inputs, preacts = forward(weights, chosen_rows, chosen_codes, LAYERS)
        feat_back, code_back, errors = backward(weights, preacts, chosen_cot, LAYERS)
        grad_terms = param_terms(inputs, errors)
        out_all = out_all.at[picked].set(outcome, mode="drop")
        feat_all = feat_all.at[picked].set(feat_back, mode="drop")
        code_all = code_all.at[picked].set(code_back, mode="drop")
        return (out_all, feat_all, code_all), grad_terms

    initial = (jnp.zeros((ROWS, D), jnp.bfloat16), jnp.zeros((ROWS, D), jnp.bfloat16), jnp.zeros((ROWS, CODE), jnp.bfloat16))
    finals, param_grad = lax.scan(per_expert, initial, (params, slot_table))
    out_rows, feat_grad, code_row_grad = finals
    code_grad = jax.ops.segment_sum(code_row_grad.astype(jnp.float32), image_ids, num_segments=IMAGES)
    return out_rows, feat_grad, param_grad, code_grad
```

```python
import jax
import jax.numpy as jnp
from jax import lax
from jax.experimental import pallas as pl
from jax.experimental.pallas import tpu as pltpu
from jax.sharding import PartitionSpec as P

LAYERS = 4
D = 512
CODE = 48
ROWS_DEV = 1024
IMG_DEV = 8
CAP = 64
PEERS = 32
NARROW = 8
LANES = 128
CHUNKS = D // LANES
TAIL = 8
BLOCK = 2 * CHUNKS * CAP + TAIL
SHARD = 262
SHARD_PAD = 264
PROWS = 2096
F32 = jnp.float32
BF16 = jnp.bfloat16
VMEM = 56 * 1024 * 1024


def params_of(semantics=None):
    return pltpu.CompilerParams(vmem_limit_bytes=VMEM, dimension_semantics=semantics)


def dot(a, b, ca=1, cb=0):
    return lax.dot_general(a, b, (((ca,), (cb,)), ((), ())), preferred_element_type=F32)


PACK_PEERS = 8


def pack_body(first_ref, routes_ref, ids_ref, feats_ref, cot_ref, out_ref, pos_ref, pos_scr, off_scr):
    step = pl.program_id(0)

    @pl.when(step == 0)
    def _():
        width = 256
        upper = (
            lax.broadcasted_iota(jnp.int32, (width, width), 0)
            <= lax.broadcasted_iota(jnp.int32, (width, width), 1)
        ).astype(F32).astype(BF16)
        expert = lax.broadcasted_iota(jnp.int32, (PEERS, width), 0)
        base = (expert * CAP - 1).astype(F32)
        carry = jnp.zeros((PEERS, 1), F32)
        for b in range(ROWS_DEV // width):
            hot = (routes_ref[:, b * width : (b + 1) * width] == expert).astype(F32)
            rank = dot(hot.astype(BF16), upper) + carry
            place = jnp.sum(hot * (rank + base), axis=0, keepdims=True)
            carry = carry + jnp.sum(hot, axis=1, keepdims=True)
            pos_scr[:, b * width : (b + 1) * width] = jnp.broadcast_to(place.astype(jnp.int32), (8, width))
        off = ids_ref[...] - first_ref[0]
        off = jnp.where(off < 0, off + PEERS * NARROW * IMG_DEV, off) + 1
        off_scr[...] = jnp.broadcast_to(off.astype(F32), (16, ROWS_DEV)).astype(BF16)
        pos_ref[...] = pos_scr[...]

    n = PACK_PEERS * CAP
    slot = lax.broadcasted_iota(jnp.int32, (n, ROWS_DEV), 0) + step * n
    pick = (pos_scr[0:1, :] == slot).astype(F32).astype(BF16)
    for half, src in enumerate((feats_ref, cot_ref)):
        got = dot(pick, src[...]).astype(BF16)
        for j in range(PACK_PEERS):
            for c in range(CHUNKS):
                r = (half * CHUNKS + c) * CAP
                out_ref[j, r : r + CAP, :] = got[j * CAP : (j + 1) * CAP, c * LANES : (c + 1) * LANES]
    tail = dot(off_scr[...], pick, 1, 1)[:TAIL]
    for j in range(PACK_PEERS):
        row = jnp.concatenate([tail[:, j * CAP : (j + 1) * CAP], jnp.zeros((TAIL, LANES - CAP), F32)], axis=1)
        out_ref[j, BLOCK - TAIL :, :] = row.astype(BF16)


def pack(first, routes, ids, feats, cot):
    whole = lambda shape: pl.BlockSpec(shape, lambda i, f: (0,) * len(shape))
    return pl.pallas_call(
        pack_body,
        grid_spec=pltpu.PrefetchScalarGridSpec(
            num_scalar_prefetch=1,
            grid=(PEERS // PACK_PEERS,),
            in_specs=[whole((1, ROWS_DEV)), whole((1, ROWS_DEV)), whole((ROWS_DEV, D)), whole((ROWS_DEV, D))],
            out_specs=[
                pl.BlockSpec((PACK_PEERS, BLOCK, LANES), lambda i, f: (i, 0, 0)),
                whole((8, ROWS_DEV)),
            ],
            scratch_shapes=[pltpu.VMEM((8, ROWS_DEV), jnp.int32), pltpu.VMEM((16, ROWS_DEV), BF16)],
        ),
        out_shape=[
            jax.ShapeDtypeStruct((PEERS, BLOCK, LANES), BF16),
            jax.ShapeDtypeStruct((8, ROWS_DEV), jnp.int32),
        ],
        compiler_params=params_of(),
        name="pack",
    )(first, routes, ids, feats, cot)


def join_body(shards_ref, out_ref, scr):
    for n in range(NARROW):
        scr[n * SHARD : (n + 1) * SHARD, :] = shards_ref[n, :SHARD, :].astype(F32)
    out_ref[...] = scr[...].astype(BF16)


def join(shards):
    return pl.pallas_call(
        join_body,
        out_shape=jax.ShapeDtypeStruct((PROWS, D), BF16),
        scratch_shapes=[pltpu.VMEM((PROWS, D), F32)],
        compiler_params=params_of(),
        name="join",
    )(shards)


EXP_PEERS = 4
EXP_ROWS = EXP_PEERS * CAP
WIN = 2 * IMG_DEV


def columns(ref, half):
    parts = []
    for c in range(CHUNKS):
        r = (half * CHUNKS + c) * CAP
        parts.append(ref[:, r : r + CAP, :].reshape(EXP_ROWS, LANES))
    return jnp.concatenate(parts, axis=1)


def store_columns(ref, half, value):
    for c in range(CHUNKS):
        r = (half * CHUNKS + c) * CAP
        ref[:, r : r + CAP, :] = value[:, c * LANES : (c + 1) * LANES].reshape(EXP_PEERS, CAP, LANES)


def expert_body(got_ref, win_ref, w_ref, out_ref, z_ref, err_ref, code_ref):
    weights = lambda l: w_ref[l * D : (l + 1) * D, :]
    code_matrix = w_ref[LAYERS * D :, :]
    rows = EXP_PEERS * WIN
    image = lax.broadcasted_iota(jnp.int32, (rows, EXP_ROWS), 0) + 1
    key = jnp.concatenate(
        [
            jnp.where(v > 0.0, v + float(j * WIN), 0.0)
            for j in range(EXP_PEERS)
            for v in [got_ref[j, BLOCK - TAIL :, :CAP].astype(F32)]
        ],
        axis=1,
    )[0:1]
    hot = (key.astype(jnp.int32) == image).astype(F32).astype(BF16)
    code_rows = dot(hot, win_ref[...], 0, 0).astype(BF16)
    code_ref[...] = code_rows

    current = columns(got_ref, 0)
    slopes = []
    for l in range(LAYERS):
        z_ref[l] = current
        pre = dot(current, weights(l))
        if l == 0:
            pre = pre + dot(code_rows, code_matrix)
        s = 0.5 * jnp.tanh(0.5 * pre) + 0.5
        act = pre * s
        slopes.append(s + act * (1.0 - s))
        current = act.astype(BF16)
    store_columns(out_ref, 0, current)
    up = columns(got_ref, 1).astype(F32)
    for l in range(LAYERS - 1, -1, -1):
        err = (up * slopes[l]).astype(BF16)
        err_ref[l] = err
        up = dot(err, weights(l), 1, 1)
    store_columns(out_ref, 1, up.astype(BF16))
    code_back = dot(err, code_matrix, 1, 1).astype(BF16)
    sums = dot(hot, code_back)
    pad = jnp.zeros((IMG_DEV, LANES // 2 - CODE), F32)
    for j in range(EXP_PEERS):
        low = sums[j * WIN : j * WIN + IMG_DEV]
        high = sums[j * WIN + IMG_DEV : (j + 1) * WIN]
        out_ref[j, BLOCK - TAIL :, :] = jnp.concatenate([low, pad, high, pad], axis=1).astype(BF16)


def expert(got, window, weights):
    rows = PEERS * CAP
    return pl.pallas_call(
        expert_body,
        grid=(PEERS // EXP_PEERS,),
        in_specs=[
            pl.BlockSpec((EXP_PEERS, BLOCK, LANES), lambda i: (i, 0, 0)),
            pl.BlockSpec((EXP_PEERS * WIN, CODE), lambda i: (i, 0)),
            pl.BlockSpec((PROWS, D), lambda i: (0, 0)),
        ],
        out_specs=[
            pl.BlockSpec((EXP_PEERS, BLOCK, LANES), lambda i: (i, 0, 0)),
            pl.BlockSpec((LAYERS, EXP_ROWS, D), lambda i: (0, i, 0)),
            pl.BlockSpec((LAYERS, EXP_ROWS, D), lambda i: (0, i, 0)),
            pl.BlockSpec((EXP_ROWS, CODE), lambda i: (i, 0)),
        ],
        out_shape=[
            jax.ShapeDtypeStruct((PEERS, BLOCK, LANES), BF16),
            jax.ShapeDtypeStruct((LAYERS, rows, D), BF16),
            jax.ShapeDtypeStruct((LAYERS, rows, D), BF16),
            jax.ShapeDtypeStruct((rows, CODE), BF16),
        ],
        compiler_params=params_of(),
        name="expert",
    )(got, window, weights)


def grads_body(z_ref, err_ref, code_ref, out_ref, scr):
    l = pl.program_id(0)
    scr[pl.ds(pl.multiple_of(l * D, D), D), :] = dot(z_ref[0], err_ref[0], 0, 0)

    @pl.when(l == 0)
    def _():
        scr[LAYERS * D :, :] = dot(code_ref[...], err_ref[0], 0, 0)

    @pl.when(l == LAYERS - 1)
    def _():
        for n in range(NARROW):
            out_ref[n, :SHARD, :] = scr[n * SHARD : (n + 1) * SHARD, :].astype(BF16)
            out_ref[n, SHARD:, :] = jnp.zeros((SHARD_PAD - SHARD, D), BF16)


def grads(z, err, code):
    rows = PEERS * CAP
    return pl.pallas_call(
        grads_body,
        grid=(LAYERS,),
        in_specs=[
            pl.BlockSpec((1, rows, D), lambda i: (i, 0, 0)),
            pl.BlockSpec((1, rows, D), lambda i: (i, 0, 0)),
            pl.BlockSpec((rows, CODE), lambda i: (0, 0)),
        ],
        out_specs=pl.BlockSpec((NARROW, SHARD_PAD, D), lambda i: (0, 0, 0)),
        out_shape=jax.ShapeDtypeStruct((NARROW, SHARD_PAD, D), BF16),
        scratch_shapes=[pltpu.VMEM((PROWS, D), F32)],
        compiler_params=params_of(),
        name="grads",
    )(z, err, code)


UNPACK_ROWS = 256


def unpack_body(pos_ref, back_ref, out_ref, feat_ref):
    place = jnp.broadcast_to(pos_ref[0:1, :].astype(F32), (LANES, UNPACK_ROWS)).T
    place = place.astype(jnp.int32)
    lane = lax.broadcasted_iota(jnp.int32, (UNPACK_ROWS, LANES), 1)
    pick = jnp.concatenate(
        [(place == lane + b * LANES).astype(F32).astype(BF16) for b in range(PEERS * CAP // LANES)], axis=1
    )
    for half, dst in enumerate((out_ref, feat_ref)):
        parts = []
        for c in range(CHUNKS):
            r = (half * CHUNKS + c) * CAP
            parts.append(back_ref[:, r : r + CAP, :].reshape(PEERS * CAP, LANES))
        dst[...] = dot(pick, jnp.concatenate(parts, axis=1)).astype(BF16)


def unpack(pos, back):
    return pl.pallas_call(
        unpack_body,
        grid=(ROWS_DEV // UNPACK_ROWS,),
        in_specs=[
            pl.BlockSpec((8, UNPACK_ROWS), lambda i: (0, i)),
            pl.BlockSpec((PEERS, BLOCK, LANES), lambda i: (0, 0, 0)),
        ],
        out_specs=[pl.BlockSpec((UNPACK_ROWS, D), lambda i: (i, 0))] * 2,
        out_shape=[jax.ShapeDtypeStruct((ROWS_DEV, D), BF16)] * 2,
        compiler_params=params_of(),
        name="unpack",
    )(pos, back)


def exchange(values):
    return lax.all_to_all(values, "expert", split_axis=0, concat_axis=0, tiled=True)


def shifted(block, axis, distance):
    devices = range(lax.axis_size(axis))
    route = [((i - distance) % len(devices), i) for i in devices]
    return lax.ppermute(block, axis, route)


def body(feats, cotangent, routes, image_ids, codes, params):
    flat = lax.axis_index(("expert", "narrow"))
    first_image = (flat * IMG_DEV).astype(jnp.int32).reshape(1)
    shards = lax.all_gather(
        jnp.pad(params[0], ((0, SHARD_PAD - SHARD), (0, 0))), "narrow", axis=0, tiled=True
    ).reshape(NARROW, SHARD_PAD, D)
    packed, pos = pack(
        first_image, routes.reshape(1, ROWS_DEV), image_ids.reshape(1, ROWS_DEV), feats, cotangent
    )
    got = exchange(packed)
    weights = join(shards)
    start = lax.axis_index("narrow") * IMG_DEV
    ring = jnp.concatenate([codes, codes[:CAP]], axis=0)
    window = lax.dynamic_slice(ring, (start, 0), (PEERS * CAP, CODE))
    window = window.reshape(PEERS, CAP, CODE)[:, :WIN].reshape(PEERS * WIN, CODE)
    reply, z, err, code_rows = expert(got, window, weights)
    back = exchange(reply)
    terms = grads(z, err, code_rows)
    mine = lax.psum_scatter(
        terms.reshape(NARROW * SHARD_PAD, D), "narrow", scatter_dimension=0, tiled=True
    )
    param_grad = mine[None, :SHARD].astype(F32)
    sums = jnp.sum(back[:, BLOCK - TAIL :, :].astype(F32), axis=0)
    high = shifted(sums[:, LANES // 2 : LANES // 2 + CODE], ("expert", "narrow"), 1)
    out_rows, feat_grad = unpack(pos, back)
    return (out_rows, feat_grad, param_grad, sums[:, :CODE] + high)


def solution(mesh):
    rows = P(("expert", "narrow"), None)
    in_specs = (rows, rows, rows, P(("expert", "narrow")), P(), P("expert", "narrow", None))
    out_specs = (rows, rows, P("expert", "narrow", None), rows)
    return jax.shard_map(body, mesh=mesh, in_specs=in_specs, out_specs=out_specs, check_vma=False)
```

```python
import jax
import jax.numpy as jnp
from jax import lax
from jax.experimental import pallas as pl
from jax.experimental.pallas import tpu as pltpu
from jax.sharding import PartitionSpec as P

LAYERS = 4
D = 512
CODE = 48
ROWS_DEV = 1024
IMG_DEV = 8
CAP = 64
PEERS = 32
NARROW = 8
LANES = 128
CHUNKS = D // LANES
TAIL = 8
BLOCK = 2 * CHUNKS * CAP + TAIL
SHARD = 262
SHARD_PAD = 264
PROWS = 2096
F32 = jnp.float32
BF16 = jnp.bfloat16
VMEM = 56 * 1024 * 1024


def params_of(semantics=None):
    return pltpu.CompilerParams(vmem_limit_bytes=VMEM, dimension_semantics=semantics)


def dot(a, b, ca=1, cb=0):
    return lax.dot_general(a, b, (((ca,), (cb,)), ((), ())), preferred_element_type=F32)


PACK_PEERS = 8


def pack_body(first_ref, routes_ref, ids_ref, feats_ref, cot_ref, out_ref, pos_ref, pos_scr, off_scr):
    step = pl.program_id(0)

    @pl.when(step == 0)
    def _():
        width = 256
        upper = (
            lax.broadcasted_iota(jnp.int32, (width, width), 0)
            <= lax.broadcasted_iota(jnp.int32, (width, width), 1)
        ).astype(F32).astype(BF16)
        expert = lax.broadcasted_iota(jnp.int32, (PEERS, width), 0)
        base = (expert * CAP - 1).astype(F32)
        carry = jnp.zeros((PEERS, 1), F32)
        for b in range(ROWS_DEV // width):
            hot = (routes_ref[:, b * width : (b + 1) * width] == expert).astype(F32)
            rank = dot(hot.astype(BF16), upper) + carry
            place = jnp.sum(hot * (rank + base), axis=0, keepdims=True)
            carry = carry + jnp.sum(hot, axis=1, keepdims=True)
            pos_scr[:, b * width : (b + 1) * width] = jnp.broadcast_to(place.astype(jnp.int32), (8, width))
        off = ids_ref[...] - first_ref[0]
        off = jnp.where(off < 0, off + PEERS * NARROW * IMG_DEV, off) + 1
        off_scr[...] = jnp.broadcast_to(off.astype(F32), (16, ROWS_DEV)).astype(BF16)
        pos_ref[...] = pos_scr[...]

    n = PACK_PEERS * CAP
    slot = lax.broadcasted_iota(jnp.int32, (n, ROWS_DEV), 0) + step * n
    pick = (pos_scr[0:1, :] == slot).astype(F32).astype(BF16)
    for half, src in enumerate((feats_ref, cot_ref)):
        got = dot(pick, src[...]).astype(BF16)
        for j in range(PACK_PEERS):
            for c in range(CHUNKS):
                r = (half * CHUNKS + c) * CAP
                out_ref[j, r : r + CAP, :] = got[j * CAP : (j + 1) * CAP, c * LANES : (c + 1) * LANES]
    tail = dot(off_scr[...], pick, 1, 1)[:TAIL]
    for j in range(PACK_PEERS):
        row = jnp.concatenate([tail[:, j * CAP : (j + 1) * CAP], jnp.zeros((TAIL, LANES - CAP), F32)], axis=1)
        out_ref[j, BLOCK - TAIL :, :] = row.astype(BF16)


def pack(first, routes, ids, feats, cot):
    whole = lambda shape: pl.BlockSpec(shape, lambda i, f: (0,) * len(shape))
    return pl.pallas_call(
        pack_body,
        grid_spec=pltpu.PrefetchScalarGridSpec(
            num_scalar_prefetch=1,
            grid=(PEERS // PACK_PEERS,),
            in_specs=[whole((1, ROWS_DEV)), whole((1, ROWS_DEV)), whole((ROWS_DEV, D)), whole((ROWS_DEV, D))],
            out_specs=[
                pl.BlockSpec((PACK_PEERS, BLOCK, LANES), lambda i, f: (i, 0, 0)),
                whole((8, ROWS_DEV)),
            ],
            scratch_shapes=[pltpu.VMEM((8, ROWS_DEV), jnp.int32), pltpu.VMEM((16, ROWS_DEV), BF16)],
        ),
        out_shape=[
            jax.ShapeDtypeStruct((PEERS, BLOCK, LANES), BF16),
            jax.ShapeDtypeStruct((8, ROWS_DEV), jnp.int32),
        ],
        compiler_params=params_of(),
        name="pack",
    )(first, routes, ids, feats, cot)


HOPS = (0, -1, 1, -2, 2, -3, 3, -4)


def join_body(narrow_ref, *refs):
    shard_refs, (out_ref, order, scr) = refs[:NARROW], refs[NARROW:]
    for hop, ref in zip(HOPS, shard_refs):
        order[(narrow_ref[0] + hop + NARROW) % NARROW] = ref[...]
    for n in range(NARROW):
        scr[n * SHARD : (n + 1) * SHARD, :] = order[n, :SHARD, :].astype(F32)
    out_ref[...] = scr[...].astype(BF16)


def join(narrow, shards):
    return pl.pallas_call(
        join_body,
        grid_spec=pltpu.PrefetchScalarGridSpec(
            num_scalar_prefetch=1,
            grid=(1,),
            in_specs=[pl.BlockSpec((SHARD_PAD, D), lambda i, n: (0, 0))] * NARROW,
            out_specs=pl.BlockSpec((PROWS, D), lambda i, n: (0, 0)),
            scratch_shapes=[pltpu.VMEM((NARROW, SHARD_PAD, D), BF16), pltpu.VMEM((PROWS, D), F32)],
        ),
        out_shape=jax.ShapeDtypeStruct((PROWS, D), BF16),
        compiler_params=params_of(),
        name="join",
    )(narrow, *shards)


EXP_PEERS = 8
EXP_ROWS = EXP_PEERS * CAP
WIN = 2 * IMG_DEV


def columns(ref, half):
    parts = []
    for c in range(CHUNKS):
        r = (half * CHUNKS + c) * CAP
        parts.append(ref[:, r : r + CAP, :].reshape(EXP_ROWS, LANES))
    return jnp.concatenate(parts, axis=1)


def store_columns(ref, half, value):
    for c in range(CHUNKS):
        r = (half * CHUNKS + c) * CAP
        ref[:, r : r + CAP, :] = value[:, c * LANES : (c + 1) * LANES].reshape(EXP_PEERS, CAP, LANES)


def expert_body(got_ref, win_ref, w_ref, out_ref, z_ref, err_ref, code_ref):
    weights = lambda l: w_ref[l * D : (l + 1) * D, :]
    code_matrix = w_ref[LAYERS * D :, :]
    rows = EXP_PEERS * WIN
    image = lax.broadcasted_iota(jnp.int32, (rows, EXP_ROWS), 0) + 1
    key = jnp.concatenate(
        [
            jnp.where(v > 0.0, v + float(j * WIN), 0.0)
            for j in range(EXP_PEERS)
            for v in [got_ref[j, BLOCK - TAIL :, :CAP].astype(F32)]
        ],
        axis=1,
    )[0:1]
    hot = (key.astype(jnp.int32) == image).astype(F32).astype(BF16)
    code_rows = dot(hot, win_ref[...], 0, 0).astype(BF16)
    code_ref[...] = code_rows

    current = columns(got_ref, 0)
    slopes = []
    for l in range(LAYERS):
        z_ref[l] = current
        pre = dot(current, weights(l))
        if l == 0:
            pre = pre + dot(code_rows, code_matrix)
        s = 0.5 * jnp.tanh(0.5 * pre) + 0.5
        act = pre * s
        slopes.append(s + act * (1.0 - s))
        current = act.astype(BF16)
    store_columns(out_ref, 0, current)
    up = columns(got_ref, 1).astype(F32)
    for l in range(LAYERS - 1, -1, -1):
        err = (up * slopes[l]).astype(BF16)
        err_ref[l] = err
        up = dot(err, weights(l), 1, 1)
    store_columns(out_ref, 1, up.astype(BF16))
    code_back = dot(err, code_matrix, 1, 1).astype(BF16)
    sums = dot(hot, code_back)
    pad = jnp.zeros((IMG_DEV, LANES // 2 - CODE), F32)
    for j in range(EXP_PEERS):
        low = sums[j * WIN : j * WIN + IMG_DEV]
        high = sums[j * WIN + IMG_DEV : (j + 1) * WIN]
        out_ref[j, BLOCK - TAIL :, :] = jnp.concatenate([low, pad, high, pad], axis=1).astype(BF16)


def expert(got, window, weights):
    rows = PEERS * CAP
    return pl.pallas_call(
        expert_body,
        grid=(PEERS // EXP_PEERS,),
        in_specs=[
            pl.BlockSpec((EXP_PEERS, BLOCK, LANES), lambda i: (i, 0, 0)),
            pl.BlockSpec((EXP_PEERS * WIN, CODE), lambda i: (i, 0)),
            pl.BlockSpec((PROWS, D), lambda i: (0, 0)),
        ],
        out_specs=[
            pl.BlockSpec((EXP_PEERS, BLOCK, LANES), lambda i: (i, 0, 0)),
            pl.BlockSpec((LAYERS, EXP_ROWS, D), lambda i: (0, i, 0)),
            pl.BlockSpec((LAYERS, EXP_ROWS, D), lambda i: (0, i, 0)),
            pl.BlockSpec((EXP_ROWS, CODE), lambda i: (i, 0)),
        ],
        out_shape=[
            jax.ShapeDtypeStruct((PEERS, BLOCK, LANES), BF16),
            jax.ShapeDtypeStruct((LAYERS, rows, D), BF16),
            jax.ShapeDtypeStruct((LAYERS, rows, D), BF16),
            jax.ShapeDtypeStruct((rows, CODE), BF16),
        ],
        compiler_params=params_of(),
        name="expert",
    )(got, window, weights)


def grads_body(narrow_ref, z_ref, err_ref, code_ref, *refs):
    out_refs, (scr, order) = refs[:NARROW], refs[NARROW:]
    l = pl.program_id(0)
    scr[pl.ds(pl.multiple_of(l * D, D), D), :] = dot(z_ref[0], err_ref[0], 0, 0)

    @pl.when(l == 0)
    def _():
        scr[LAYERS * D :, :] = dot(code_ref[...], err_ref[0], 0, 0)

    @pl.when(l == LAYERS - 1)
    def _():
        for n in range(NARROW):
            order[n, :SHARD, :] = scr[n * SHARD : (n + 1) * SHARD, :].astype(BF16)
            order[n, SHARD:, :] = jnp.zeros((SHARD_PAD - SHARD, D), BF16)
        for k, ref in enumerate(out_refs):
            ref[...] = order[(narrow_ref[0] + k) % NARROW]


def grads(narrow, z, err, code):
    rows = PEERS * CAP
    return pl.pallas_call(
        grads_body,
        grid_spec=pltpu.PrefetchScalarGridSpec(
            num_scalar_prefetch=1,
            grid=(LAYERS,),
            in_specs=[
                pl.BlockSpec((1, rows, D), lambda i, n: (i, 0, 0)),
                pl.BlockSpec((1, rows, D), lambda i, n: (i, 0, 0)),
                pl.BlockSpec((rows, CODE), lambda i, n: (0, 0)),
            ],
            out_specs=[pl.BlockSpec((SHARD_PAD, D), lambda i, n: (0, 0))] * NARROW,
            scratch_shapes=[pltpu.VMEM((PROWS, D), F32), pltpu.VMEM((NARROW, SHARD_PAD, D), BF16)],
        ),
        out_shape=[jax.ShapeDtypeStruct((SHARD_PAD, D), BF16)] * NARROW,
        compiler_params=params_of(),
        name="grads",
    )(narrow, z, err, code)


UNPACK_ROWS = 256


def unpack_body(pos_ref, back_ref, out_ref, feat_ref):
    place = jnp.broadcast_to(pos_ref[0:1, :].astype(F32), (LANES, UNPACK_ROWS)).T
    place = place.astype(jnp.int32)
    lane = lax.broadcasted_iota(jnp.int32, (UNPACK_ROWS, LANES), 1)
    pick = jnp.concatenate(
        [(place == lane + b * LANES).astype(F32).astype(BF16) for b in range(PEERS * CAP // LANES)], axis=1
    )
    for half, dst in enumerate((out_ref, feat_ref)):
        parts = []
        for c in range(CHUNKS):
            r = (half * CHUNKS + c) * CAP
            parts.append(back_ref[:, r : r + CAP, :].reshape(PEERS * CAP, LANES))
        dst[...] = dot(pick, jnp.concatenate(parts, axis=1)).astype(BF16)


def unpack(pos, back):
    return pl.pallas_call(
        unpack_body,
        grid=(ROWS_DEV // UNPACK_ROWS,),
        in_specs=[
            pl.BlockSpec((8, UNPACK_ROWS), lambda i: (0, i)),
            pl.BlockSpec((PEERS, BLOCK, LANES), lambda i: (0, 0, 0)),
        ],
        out_specs=[pl.BlockSpec((UNPACK_ROWS, D), lambda i: (i, 0))] * 2,
        out_shape=[jax.ShapeDtypeStruct((ROWS_DEV, D), BF16)] * 2,
        compiler_params=params_of(),
        name="unpack",
    )(pos, back)


def exchange(values):
    return lax.all_to_all(values, "expert", split_axis=0, concat_axis=0, tiled=True)


def shifted(block, axis, distance):
    devices = range(lax.axis_size(axis))
    route = [((i - distance) % len(devices), i) for i in devices]
    return lax.ppermute(block, axis, route)


def ring_gather(own):
    got = [own]
    ahead = behind = own
    for step in range(1, NARROW // 2 + 1):
        ahead = shifted(ahead, "narrow", 1)
        got.append(ahead)
        if step < NARROW // 2:
            behind = shifted(behind, "narrow", -1)
            got.append(behind)
    return got


def ring_reduce(terms):
    add = lambda a, b: a.astype(F32) + b.astype(F32)
    half = NARROW // 2
    ahead, behind = terms[half], terms[half + 1]
    for step in range(half):
        ahead = shifted(ahead, "narrow", 1)
        if step > 0:
            behind = shifted(behind, "narrow", -1)
        if step < half - 1:
            ahead = add(ahead, terms[half - 1 - step]).astype(BF16)
            if step > 0:
                behind = add(behind, terms[half + 1 + step]).astype(BF16)
    return add(ahead, behind) + terms[0].astype(F32)


def body(feats, cotangent, routes, image_ids, codes, params):
    flat = lax.axis_index(("expert", "narrow"))
    first_image = (flat * IMG_DEV).astype(jnp.int32).reshape(1)
    narrow = lax.axis_index("narrow").astype(jnp.int32)
    packed, pos = pack(
        first_image, routes.reshape(1, ROWS_DEV), image_ids.reshape(1, ROWS_DEV), feats, cotangent
    )
    got = exchange(packed)
    shards = ring_gather(jnp.pad(params[0], ((0, SHARD_PAD - SHARD), (0, 0))))
    weights = join(narrow.reshape(1), shards)
    ring = jnp.concatenate([codes, codes[:CAP]], axis=0)
    window = lax.dynamic_slice(ring, (narrow * IMG_DEV, 0), (PEERS * CAP, CODE))
    window = window.reshape(PEERS, CAP, CODE)[:, :WIN].reshape(PEERS * WIN, CODE)
    reply, z, err, code_rows = expert(got, window, weights)
    back = exchange(reply)
    mine = ring_reduce(grads(narrow.reshape(1), z, err, code_rows))
    param_grad = mine[None, :SHARD]
    sums = jnp.sum(back[:, BLOCK - TAIL :, :].astype(F32), axis=0)
    high = shifted(sums[:, LANES // 2 : LANES // 2 + CODE], ("expert", "narrow"), 1)
    out_rows, feat_grad = unpack(pos, back)
    return (out_rows, feat_grad, param_grad, sums[:, :CODE] + high)


def solution(mesh):
    rows = P(("expert", "narrow"), None)
    in_specs = (rows, rows, rows, P(("expert", "narrow")), P(), P("expert", "narrow", None))
    out_specs = (rows, rows, P("expert", "narrow", None), rows)
    return jax.shard_map(body, mesh=mesh, in_specs=in_specs, out_specs=out_specs, check_vma=False)
```

```python
import jax
import jax.numpy as jnp
from jax import lax
from jax.experimental import pallas as pl
from jax.experimental.pallas import tpu as pltpu
from jax.sharding import PartitionSpec as P

LAYERS = 4
D = 512
CODE = 48
ROWS_DEV = 1024
IMG_DEV = 8
CAP = 64
PEERS = 32
NARROW = 8
LANES = 128
CHUNKS = D // LANES
TAIL = 8
BLOCK = 2 * CHUNKS * CAP + TAIL
SHARD = 262
SHARD_PAD = 264
PROWS = 2096
F32 = jnp.float32
BF16 = jnp.bfloat16
MIB = 1024 * 1024


def params_of(mib):
    return pltpu.CompilerParams(vmem_limit_bytes=mib * MIB)


def cost(us):
    return pl.CostEstimate(flops=0, transcendentals=0, bytes_accessed=us * 3_000_000)


def in_vmem():
    return pl.BlockSpec(memory_space=pltpu.VMEM)


def in_smem():
    return pl.BlockSpec(memory_space=pltpu.SMEM)


def in_hbm():
    return pl.BlockSpec(memory_space=pltpu.HBM)


def pinned(*values):
    return [pltpu.with_memory_space_constraint(v, pltpu.HBM) for v in values]


def dot(a, b, ca=1, cb=0):
    return lax.dot_general(a, b, (((ca,), (cb,)), ((), ())), preferred_element_type=F32)


SLOTS = PEERS * CAP
PACK_PEERS = 4


def column_of(half, c):
    r = (half * CHUNKS + c) * CAP
    return slice(r, r + CAP)


def pack_body(
    first_ref, routes_hbm, ids_hbm, feats_hbm, cot_hbm, out_hbm, pos_ref, routes_ref, ids_ref, feats_ref, cot_ref, out_ref, sems
):
    sources = (feats_ref, cot_ref)
    small, loads = [
        [pltpu.make_async_copy(hbm, ref, sems.at[i]) for i, hbm, ref in group]
        for group in (
            ((0, routes_hbm, routes_ref), (1, ids_hbm, ids_ref)),
            ((2, feats_hbm, feats_ref), (3, cot_hbm, cot_ref)),
        )
    ]
    for load in small + loads:
        load.start()
    for load in small:
        load.wait()
    width = 256
    upper = (
        lax.broadcasted_iota(jnp.int32, (width, width), 0)
        <= lax.broadcasted_iota(jnp.int32, (width, width), 1)
    ).astype(F32).astype(BF16)
    expert = lax.broadcasted_iota(jnp.int32, (PEERS, width), 0)
    base = (expert * CAP - 1).astype(F32)
    carry = jnp.zeros((PEERS, 1), F32)
    tail = jnp.zeros((PEERS, CAP), F32)
    off = ids_ref[...] - first_ref[0]
    off = (jnp.where(off < 0, off + PEERS * NARROW * IMG_DEV, off) + 1).astype(F32)
    for b in range(ROWS_DEV // width):
        part = slice(b * width, (b + 1) * width)
        hot = (routes_ref[:, part] == expert).astype(F32)
        rank = dot(hot.astype(BF16), upper) + carry
        carry = carry + jnp.sum(hot, axis=1, keepdims=True)
        pos_ref[:, part] = jnp.sum(hot * (rank + base), axis=0, keepdims=True).astype(jnp.int32)
        slot = jnp.sum(hot * rank, axis=0, keepdims=True).astype(jnp.int32) - 1
        at = (lax.broadcasted_iota(jnp.int32, (CAP, width), 0) == slot).astype(F32).astype(BF16)
        tail = tail + dot((hot * off[:, part]).astype(BF16), at, 1, 1)
    tail = jnp.concatenate([tail, jnp.zeros((PEERS, LANES - CAP), F32)], axis=1)
    n = PACK_PEERS * CAP
    stores = []
    for g in range(PEERS // PACK_PEERS):
        peers = slice(g * PACK_PEERS, (g + 1) * PACK_PEERS)
        slot = lax.broadcasted_iota(jnp.int32, (n, ROWS_DEV), 0) + g * n
        pick = (pos_ref[...] == slot).astype(F32).astype(BF16)
        for half, src in enumerate(sources):
            if g == 0:
                loads[half].wait()
            got = dot(pick, src[...]).astype(BF16)
            for c in range(CHUNKS):
                out_ref[peers, column_of(half, c), :] = got[:, c * LANES : (c + 1) * LANES].reshape(
                    PACK_PEERS, CAP, LANES
                )
        for e in range(g * PACK_PEERS, (g + 1) * PACK_PEERS):
            out_ref[e, BLOCK - TAIL :, :] = jnp.broadcast_to(tail[e : e + 1], (TAIL, LANES)).astype(BF16)
        stores.append(pltpu.make_async_copy(out_ref.at[peers], out_hbm.at[peers], sems.at[4 + g]))
        stores[-1].start()
    for store in stores:
        store.wait()


def pack(first, routes, ids, feats, cot):
    return pl.pallas_call(
        pack_body,
        in_specs=[in_smem()] + [in_hbm()] * 4,
        out_specs=[in_hbm(), in_vmem()],
        scratch_shapes=[
            pltpu.VMEM((1, ROWS_DEV), jnp.int32),
            pltpu.VMEM((1, ROWS_DEV), jnp.int32),
            pltpu.VMEM((ROWS_DEV, D), BF16),
            pltpu.VMEM((ROWS_DEV, D), BF16),
            pltpu.VMEM((PEERS, BLOCK, LANES), BF16),
            pltpu.SemaphoreType.DMA((4 + PEERS // PACK_PEERS,)),
        ],
        out_shape=[
            pltpu.HBM((PEERS, BLOCK, LANES), BF16),
            jax.ShapeDtypeStruct((1, ROWS_DEV), jnp.int32),
        ],
        compiler_params=params_of(32),
        cost_estimate=cost(8),
        name="pack",
    )(first, *pinned(routes, ids, feats, cot))


HOPS = (0, -1, 1, -2, 2, -3, 3, -4)


def join_body(narrow_ref, *refs):
    shard_refs, (out_ref, order, scr) = refs[:NARROW], refs[NARROW:]
    for hop, ref in zip(HOPS, shard_refs):
        order[(narrow_ref[0] + hop + NARROW) % NARROW] = ref[...]
    for n in range(NARROW):
        scr[n * SHARD : (n + 1) * SHARD, :] = order[n, :SHARD, :].astype(F32)
    out_ref[...] = scr[...].astype(BF16)


def join(narrow, shards):
    return pl.pallas_call(
        join_body,
        in_specs=[in_smem()] + [in_vmem()] * NARROW,
        out_specs=in_vmem(),
        scratch_shapes=[pltpu.VMEM((NARROW, SHARD_PAD, D), BF16), pltpu.VMEM((PROWS, D), F32)],
        out_shape=jax.ShapeDtypeStruct((PROWS, D), BF16),
        compiler_params=params_of(12),
        cost_estimate=cost(4),
        name="join",
    )(narrow, *shards)


EXP_PEERS = 16
EXP_ROWS = EXP_PEERS * CAP
EXP_STEPS = PEERS // EXP_PEERS
WIN = 2 * IMG_DEV


def expert_body(
    got_hbm, win_ref, w_ref, out_hbm, z_hbm, err_hbm, code_ref, got_ref, out_ref, z_ref, err_ref, loads, stores, z_sems, err_sems
):
    weights = lambda l: w_ref[l * D : (l + 1) * D, :]
    code_matrix = w_ref[LAYERS * D :, :]
    all_peers = [slice(k * EXP_PEERS, (k + 1) * EXP_PEERS) for k in range(EXP_STEPS)]
    inputs = [pltpu.make_async_copy(got_hbm.at[p], got_ref.at[p], loads.at[k]) for k, p in enumerate(all_peers)]
    for load in inputs:
        load.start()
    outputs = []
    pending = {}
    for k, peers in enumerate(all_peers):
        span = slice(k * EXP_ROWS, (k + 1) * EXP_ROWS)
        buf = k % 2

        def save(kind, ref, hbm, sems, l, value):
            if (kind, buf, l) in pending:
                pending[kind, buf, l].wait()
            ref[buf, l] = value
            pending[kind, buf, l] = pltpu.make_async_copy(ref.at[buf, l], hbm.at[l, span], sems.at[buf, l])
            pending[kind, buf, l].start()

        def columns(half):
            parts = [got_ref[peers, column_of(half, c), :].reshape(EXP_ROWS, LANES) for c in range(CHUNKS)]
            return jnp.concatenate(parts, axis=1)

        def store_columns(half, value):
            for c in range(CHUNKS):
                out_ref[peers, column_of(half, c), :] = value[:, c * LANES : (c + 1) * LANES].reshape(
                    EXP_PEERS, CAP, LANES
                )

        inputs[k].wait()
        image = lax.broadcasted_iota(jnp.int32, (EXP_PEERS * WIN, EXP_ROWS), 0) + 1
        key = jnp.concatenate(
            [
                jnp.where(v > 0.0, v + float(j * WIN), 0.0)
                for j in range(EXP_PEERS)
                for v in [got_ref[k * EXP_PEERS + j, BLOCK - TAIL :, :CAP].astype(F32)]
            ],
            axis=1,
        )[0:1]
        hot = (key.astype(jnp.int32) == image).astype(F32).astype(BF16)
        window = win_ref[k * EXP_PEERS * WIN : (k + 1) * EXP_PEERS * WIN, :]
        code_rows = dot(hot, window, 0, 0).astype(BF16)
        code_ref[span, :] = code_rows
        current = columns(0)
        slopes = []
        for l in range(LAYERS):
            save("z", z_ref, z_hbm, z_sems, l, current)
            pre = dot(current, weights(l))
            if l == 0:
                pre = pre + dot(code_rows, code_matrix)
            s = 0.5 * jnp.tanh(0.5 * pre) + 0.5
            act = pre * s
            slopes.append(s + act * (1.0 - s))
            current = act.astype(BF16)
        store_columns(0, current)
        up = columns(1).astype(F32)
        for l in range(LAYERS - 1, -1, -1):
            err = (up * slopes[l]).astype(BF16)
            save("err", err_ref, err_hbm, err_sems, l, err)
            up = dot(err, weights(l), 1, 1)
        code_back = dot(err, code_matrix, 1, 1).astype(BF16)
        store_columns(1, up.astype(BF16))
        sums = dot(hot, code_back)
        pad = jnp.zeros((IMG_DEV, LANES // 2 - CODE), F32)
        for j in range(EXP_PEERS):
            low = sums[j * WIN : j * WIN + IMG_DEV]
            high = sums[j * WIN + IMG_DEV : (j + 1) * WIN]
            out_ref[k * EXP_PEERS + j, BLOCK - TAIL :, :] = jnp.concatenate([low, pad, high, pad], axis=1).astype(BF16)
        outputs.append(pltpu.make_async_copy(out_ref.at[peers], out_hbm.at[peers], stores.at[k]))
        outputs[-1].start()
    for store in list(pending.values()) + outputs:
        store.wait()


def expert(got, window, weights):
    return pl.pallas_call(
        expert_body,
        in_specs=[in_hbm(), in_vmem(), in_vmem()],
        out_specs=[in_hbm(), in_hbm(), in_hbm(), in_vmem()],
        scratch_shapes=[
            pltpu.VMEM((PEERS, BLOCK, LANES), BF16),
            pltpu.VMEM((PEERS, BLOCK, LANES), BF16),
            pltpu.VMEM((2, LAYERS, EXP_ROWS, D), BF16),
            pltpu.VMEM((2, LAYERS, EXP_ROWS, D), BF16),
            pltpu.SemaphoreType.DMA((EXP_STEPS,)),
            pltpu.SemaphoreType.DMA((EXP_STEPS,)),
            pltpu.SemaphoreType.DMA((2, LAYERS)),
            pltpu.SemaphoreType.DMA((2, LAYERS)),
        ],
        out_shape=[
            pltpu.HBM((PEERS, BLOCK, LANES), BF16),
            pltpu.HBM((LAYERS, SLOTS, D), BF16),
            pltpu.HBM((LAYERS, SLOTS, D), BF16),
            jax.ShapeDtypeStruct((SLOTS, CODE), BF16),
        ],
        compiler_params=params_of(44),
        cost_estimate=cost(17),
        name="expert",
    )(*pinned(got), window, weights)


def grads_body(narrow_ref, z_ref, err_ref, code_ref, *refs):
    out_refs, (scr, order) = refs[:NARROW], refs[NARROW:]
    l = pl.program_id(0)
    scr[pl.ds(pl.multiple_of(l * D, D), D), :] = dot(z_ref[0], err_ref[0], 0, 0)

    @pl.when(l == 0)
    def _():
        scr[LAYERS * D :, :] = dot(code_ref[...], err_ref[0], 0, 0)

    @pl.when(l == LAYERS - 1)
    def _():
        for n in range(NARROW):
            order[n, :SHARD, :] = scr[n * SHARD : (n + 1) * SHARD, :].astype(BF16)
            order[n, SHARD:, :] = jnp.zeros((SHARD_PAD - SHARD, D), BF16)
        for k, ref in enumerate(out_refs):
            ref[...] = order[(narrow_ref[0] + k) % NARROW]


def grads(narrow, z, err, code):
    rows = PEERS * CAP
    return pl.pallas_call(
        grads_body,
        grid_spec=pltpu.PrefetchScalarGridSpec(
            num_scalar_prefetch=1,
            grid=(LAYERS,),
            in_specs=[
                pl.BlockSpec((1, rows, D), lambda i, n: (i, 0, 0)),
                pl.BlockSpec((1, rows, D), lambda i, n: (i, 0, 0)),
                pl.BlockSpec((rows, CODE), lambda i, n: (0, 0)),
            ],
            out_specs=[pl.BlockSpec((SHARD_PAD, D), lambda i, n: (0, 0))] * NARROW,
            scratch_shapes=[pltpu.VMEM((PROWS, D), F32), pltpu.VMEM((NARROW, SHARD_PAD, D), BF16)],
        ),
        out_shape=[jax.ShapeDtypeStruct((SHARD_PAD, D), BF16)] * NARROW,
        compiler_params=params_of(40),
        cost_estimate=cost(10),
        name="grads",
    )(narrow, z, err, code)


TILE = 8
UNROLL = 32
UNPACK_PEERS = 4
UNPACK_ROWS = 256


def unpack_body(pos_ref, back_hbm, out_hbm, feat_hbm, back_ref, slots, rows, out_ref, feat_ref, loads, sems):
    all_peers = [slice(k, k + UNPACK_PEERS) for k in range(0, PEERS, UNPACK_PEERS)]
    inputs = [pltpu.make_async_copy(back_hbm.at[p], back_ref.at[p], loads.at[k]) for k, p in enumerate(all_peers)]
    for load in inputs:
        load.start()
    n = UNPACK_PEERS * CAP
    for k, peers in enumerate(all_peers):
        inputs[k].wait()
        for half in range(2):
            for c in range(CHUNKS):
                got = back_ref[peers, column_of(half, c), :].reshape(n, LANES).astype(F32)
                slots[pl.ds(k * n * TILE + half * CHUNKS + c, n, stride=TILE), :] = got
    stores = []
    for part in range(ROWS_DEV // UNPACK_ROWS):
        span = slice(part * UNPACK_ROWS, (part + 1) * UNPACK_ROWS)

        def move(i, _):
            for u in range(UNROLL):
                r = part * UNPACK_ROWS + i * UNROLL + u
                p = pos_ref[0, r]
                rows[pl.ds(pl.multiple_of(r * TILE, TILE), TILE), :] = slots[
                    pl.ds(pl.multiple_of(p * TILE, TILE), TILE), :
                ]
            return 0

        lax.fori_loop(0, UNPACK_ROWS // UNROLL, move, 0)
        for half, (dst, hbm) in enumerate(((out_ref, out_hbm), (feat_ref, feat_hbm))):
            for c in range(CHUNKS):
                dst[span, c * LANES : (c + 1) * LANES] = rows[
                    pl.ds(part * UNPACK_ROWS * TILE + half * CHUNKS + c, UNPACK_ROWS, stride=TILE), :
                ].astype(BF16)
            store = pltpu.make_async_copy(dst.at[span], hbm.at[span], sems.at[part, half])
            store.start()
            stores.append(store)
    for store in stores:
        store.wait()


def unpack(pos, back):
    return pl.pallas_call(
        unpack_body,
        in_specs=[in_smem(), in_hbm()],
        out_specs=[in_hbm()] * 2,
        scratch_shapes=[
            pltpu.VMEM((PEERS, BLOCK, LANES), BF16),
            pltpu.VMEM((SLOTS * TILE, LANES), F32),
            pltpu.VMEM((ROWS_DEV * TILE, LANES), F32),
            pltpu.VMEM((ROWS_DEV, D), BF16),
            pltpu.VMEM((ROWS_DEV, D), BF16),
            pltpu.SemaphoreType.DMA((PEERS // UNPACK_PEERS,)),
            pltpu.SemaphoreType.DMA((ROWS_DEV // UNPACK_ROWS, 2)),
        ],
        out_shape=[pltpu.HBM((ROWS_DEV, D), BF16)] * 2,
        compiler_params=params_of(32),
        cost_estimate=cost(7),
        name="unpack",
    )(pos, *pinned(back))


def exchange(values):
    return lax.all_to_all(values, "expert", split_axis=0, concat_axis=0, tiled=True)


def shifted(block, axis, distance):
    devices = range(lax.axis_size(axis))
    route = [((i - distance) % len(devices), i) for i in devices]
    return lax.ppermute(block, axis, route)


def ring_gather(own):
    got = [own]
    ahead = behind = own
    for step in range(1, NARROW // 2 + 1):
        ahead = shifted(ahead, "narrow", 1)
        got.append(ahead)
        if step < NARROW // 2:
            behind = shifted(behind, "narrow", -1)
            got.append(behind)
    return got


def ring_reduce(terms):
    add = lambda a, b: a.astype(F32) + b.astype(F32)
    half = NARROW // 2
    ahead, behind = terms[half], terms[half + 1]
    for step in range(half):
        ahead = shifted(ahead, "narrow", 1)
        if step > 0:
            behind = shifted(behind, "narrow", -1)
        if step < half - 1:
            ahead = add(ahead, terms[half - 1 - step]).astype(BF16)
            if step > 0:
                behind = add(behind, terms[half + 1 + step]).astype(BF16)
    return finish(ahead, behind, terms[0])


def finish_body(a_ref, b_ref, c_ref, out_ref):
    total = a_ref[...].astype(F32) + b_ref[...].astype(F32) + c_ref[...].astype(F32)
    out_ref[:, 0, :] = total[:SHARD]


def finish(a, b, c):
    return pl.pallas_call(
        finish_body,
        in_specs=[in_vmem()] * 3,
        out_specs=in_vmem(),
        out_shape=jax.ShapeDtypeStruct((SHARD, 1, D), F32),
        compiler_params=params_of(8),
        cost_estimate=cost(2),
        name="finish",
    )(a, b, c)


def body(feats, cotangent, routes, image_ids, codes, params):
    flat = lax.axis_index(("expert", "narrow"))
    first_image = (flat * IMG_DEV).astype(jnp.int32).reshape(1)
    narrow = lax.axis_index("narrow").astype(jnp.int32)
    packed, pos = pack(
        first_image, routes.reshape(1, ROWS_DEV), image_ids.reshape(1, ROWS_DEV), feats, cotangent
    )
    got = exchange(packed)
    shards = ring_gather(jnp.pad(params[0], ((0, SHARD_PAD - SHARD), (0, 0))))
    weights = join(narrow.reshape(1), shards)
    ring = jnp.concatenate([codes, codes[:CAP]], axis=0)
    window = lax.dynamic_slice(ring, (narrow * IMG_DEV, 0), (PEERS * CAP, CODE))
    window = window.reshape(PEERS, CAP, CODE)[:, :WIN].reshape(PEERS * WIN, CODE)
    reply, z, err, code_rows = expert(got, window, weights)
    back = exchange(reply)
    mine = ring_reduce(grads(narrow.reshape(1), z, err, code_rows))
    back, mine = lax.optimization_barrier((back, mine))
    param_grad = mine.transpose(1, 0, 2)
    sums = jnp.sum(back[:, BLOCK - TAIL :, :].astype(F32), axis=0)
    high = shifted(sums[:, LANES // 2 : LANES // 2 + CODE], ("expert", "narrow"), 1)
    out_rows, feat_grad = unpack(pos, back)
    return (out_rows, feat_grad, param_grad, sums[:, :CODE] + high)


def solution(mesh):
    rows = P(("expert", "narrow"), None)
    in_specs = (rows, rows, rows, P(("expert", "narrow")), P(), P("expert", "narrow", None))
    out_specs = (rows, rows, P("expert", "narrow", None), rows)
    return jax.shard_map(body, mesh=mesh, in_specs=in_specs, out_specs=out_specs, check_vma=False)
```

```python
import jax
import jax.numpy as jnp
from jax import lax
from jax.experimental import pallas as pl
from jax.experimental.pallas import tpu as pltpu
from jax.sharding import PartitionSpec as P

LAYERS = 4
D = 512
CODE = 48
ROWS_DEV = 1024
IMG_DEV = 8
CAP = 64
PEERS = 32
NARROW = 8
LANES = 128
CHUNKS = D // LANES
TAIL = 8
BLOCK = 2 * CHUNKS * CAP + TAIL
SHARD = 262
SHARD_PAD = 264
PROWS = 2096
F32 = jnp.float32
BF16 = jnp.bfloat16
MIB = 1024 * 1024


def params_of(mib):
    return pltpu.CompilerParams(vmem_limit_bytes=mib * MIB)


def cost(us):
    return pl.CostEstimate(flops=0, transcendentals=0, bytes_accessed=us * 3_000_000)


def in_vmem():
    return pl.BlockSpec(memory_space=pltpu.VMEM)


def in_smem():
    return pl.BlockSpec(memory_space=pltpu.SMEM)


def in_hbm():
    return pl.BlockSpec(memory_space=pltpu.HBM)


def pinned(*values):
    return [pltpu.with_memory_space_constraint(v, pltpu.HBM) for v in values]


def dot(a, b, ca=1, cb=0):
    return lax.dot_general(a, b, (((ca,), (cb,)), ((), ())), preferred_element_type=F32)


SLOTS = PEERS * CAP
PACK_PEERS = 4


def column_of(half, c):
    r = (half * CHUNKS + c) * CAP
    return slice(r, r + CAP)


def pack_body(
    first_ref, routes_hbm, ids_hbm, feats_hbm, cot_hbm, out_hbm, pos_ref, routes_ref, ids_ref, feats_ref, cot_ref, out_ref, sems
):
    sources = (feats_ref, cot_ref)
    small, loads = [
        [pltpu.make_async_copy(hbm, ref, sems.at[i]) for i, hbm, ref in group]
        for group in (
            ((0, routes_hbm, routes_ref), (1, ids_hbm, ids_ref)),
            ((2, feats_hbm, feats_ref), (3, cot_hbm, cot_ref)),
        )
    ]
    for load in small + loads:
        load.start()
    for load in small:
        load.wait()
    width = 256
    upper = (
        lax.broadcasted_iota(jnp.int32, (width, width), 0)
        <= lax.broadcasted_iota(jnp.int32, (width, width), 1)
    ).astype(F32).astype(BF16)
    expert = lax.broadcasted_iota(jnp.int32, (PEERS, width), 0)
    base = (expert * CAP - 1).astype(F32)
    carry = jnp.zeros((PEERS, 1), F32)
    tail = jnp.zeros((PEERS, CAP), F32)
    off = ids_ref[...] - first_ref[0]
    off = (jnp.where(off < 0, off + PEERS * NARROW * IMG_DEV, off) + 1).astype(F32)
    for b in range(ROWS_DEV // width):
        part = slice(b * width, (b + 1) * width)
        hot = (routes_ref[:, part] == expert).astype(F32)
        rank = dot(hot.astype(BF16), upper) + carry
        carry = carry + jnp.sum(hot, axis=1, keepdims=True)
        pos_ref[:, part] = jnp.sum(hot * (rank + base), axis=0, keepdims=True).astype(jnp.int32)
        slot = jnp.sum(hot * rank, axis=0, keepdims=True).astype(jnp.int32) - 1
        at = (lax.broadcasted_iota(jnp.int32, (CAP, width), 0) == slot).astype(F32).astype(BF16)
        tail = tail + dot((hot * off[:, part]).astype(BF16), at, 1, 1)
    tail = jnp.concatenate([tail, jnp.zeros((PEERS, LANES - CAP), F32)], axis=1)
    n = PACK_PEERS * CAP
    stores = []
    for g in range(PEERS // PACK_PEERS):
        peers = slice(g * PACK_PEERS, (g + 1) * PACK_PEERS)
        slot = lax.broadcasted_iota(jnp.int32, (n, ROWS_DEV), 0) + g * n
        pick = (pos_ref[...] == slot).astype(F32).astype(BF16)
        for half, src in enumerate(sources):
            if g == 0:
                loads[half].wait()
            got = dot(pick, src[...]).astype(BF16)
            for c in range(CHUNKS):
                out_ref[peers, column_of(half, c), :] = got[:, c * LANES : (c + 1) * LANES].reshape(
                    PACK_PEERS, CAP, LANES
                )
        for e in range(g * PACK_PEERS, (g + 1) * PACK_PEERS):
            out_ref[e, BLOCK - TAIL :, :] = jnp.broadcast_to(tail[e : e + 1], (TAIL, LANES)).astype(BF16)
        stores.append(pltpu.make_async_copy(out_ref.at[peers], out_hbm.at[peers], sems.at[4 + g]))
        stores[-1].start()
    for store in stores:
        store.wait()


def pack(first, routes, ids, feats, cot):
    return pl.pallas_call(
        pack_body,
        in_specs=[in_smem()] + [in_hbm()] * 4,
        out_specs=[in_hbm(), in_vmem()],
        scratch_shapes=[
            pltpu.VMEM((1, ROWS_DEV), jnp.int32),
            pltpu.VMEM((1, ROWS_DEV), jnp.int32),
            pltpu.VMEM((ROWS_DEV, D), BF16),
            pltpu.VMEM((ROWS_DEV, D), BF16),
            pltpu.VMEM((PEERS, BLOCK, LANES), BF16),
            pltpu.SemaphoreType.DMA((4 + PEERS // PACK_PEERS,)),
        ],
        out_shape=[
            pltpu.HBM((PEERS, BLOCK, LANES), BF16),
            jax.ShapeDtypeStruct((1, ROWS_DEV), jnp.int32),
        ],
        compiler_params=params_of(32),
        cost_estimate=cost(8),
        name="pack",
    )(first, *pinned(routes, ids, feats, cot))


HOPS = (0, -1, 1, -2, 2, -3, 3, -4)


def join_body(narrow_ref, *refs):
    shard_refs, (out_ref, order, scr) = refs[:NARROW], refs[NARROW:]
    for hop, ref in zip(HOPS, shard_refs):
        order[(narrow_ref[0] + hop + NARROW) % NARROW] = ref[...]
    for n in range(NARROW):
        scr[n * SHARD : (n + 1) * SHARD, :] = order[n, :SHARD, :].astype(F32)
    out_ref[...] = scr[...].astype(BF16)


def join(narrow, shards):
    return pl.pallas_call(
        join_body,
        in_specs=[in_smem()] + [in_vmem()] * NARROW,
        out_specs=in_vmem(),
        scratch_shapes=[pltpu.VMEM((NARROW, SHARD_PAD, D), BF16), pltpu.VMEM((PROWS, D), F32)],
        out_shape=jax.ShapeDtypeStruct((PROWS, D), BF16),
        compiler_params=params_of(12),
        cost_estimate=cost(4),
        name="join",
    )(narrow, *shards)


EXP_PEERS = 16
EXP_ROWS = EXP_PEERS * CAP
EXP_STEPS = PEERS // EXP_PEERS
WIN = 2 * IMG_DEV


def expert_body(
    got_hbm, win_ref, w_ref, out_hbm, z_hbm, err_hbm, code_ref, got_ref, out_ref, z_ref, err_ref, loads, stores
):
    weights = lambda l: w_ref[l * D : (l + 1) * D, :]
    code_matrix = w_ref[LAYERS * D :, :]
    all_peers = [slice(k * EXP_PEERS, (k + 1) * EXP_PEERS) for k in range(EXP_STEPS)]
    half_block = CHUNKS * CAP
    parts = (slice(0, half_block), slice(2 * half_block, BLOCK), slice(half_block, 2 * half_block))
    inputs = [
        [
            pltpu.make_async_copy(got_hbm.at[peers, part], got_ref.at[peers, part], loads.at[k, i])
            for i, part in enumerate(parts)
        ]
        for k, peers in enumerate(all_peers)
    ]
    for group in inputs:
        for load in group:
            load.start()
    outputs = []

    def save(k, i, src, dst):
        outputs.append(pltpu.make_async_copy(src, dst, stores.at[k, i]))
        outputs[-1].start()

    for k, peers in enumerate(all_peers):
        span = slice(k * EXP_ROWS, (k + 1) * EXP_ROWS)

        def columns(half):
            cols = [got_ref[peers, column_of(half, c), :].reshape(EXP_ROWS, LANES) for c in range(CHUNKS)]
            return jnp.concatenate(cols, axis=1)

        def store_columns(half, value):
            for c in range(CHUNKS):
                out_ref[peers, column_of(half, c), :] = value[:, c * LANES : (c + 1) * LANES].reshape(
                    EXP_PEERS, CAP, LANES
                )

        inputs[k][0].wait()
        inputs[k][1].wait()
        image = lax.broadcasted_iota(jnp.int32, (EXP_PEERS * WIN, EXP_ROWS), 0) + 1
        key = jnp.concatenate(
            [
                jnp.where(v > 0.0, v + float(j * WIN), 0.0)
                for j in range(EXP_PEERS)
                for v in [got_ref[k * EXP_PEERS + j, BLOCK - TAIL :, :CAP].astype(F32)]
            ],
            axis=1,
        )[0:1]
        hot = (key.astype(jnp.int32) == image).astype(F32).astype(BF16)
        window = win_ref[k * EXP_PEERS * WIN : (k + 1) * EXP_PEERS * WIN, :]
        code_rows = dot(hot, window, 0, 0).astype(BF16)
        code_ref[span, :] = code_rows
        current = columns(0)
        slopes = []
        for l in range(LAYERS):
            z_ref[l, span, :] = current
            if l == 0:
                pre = dot(code_rows, code_matrix) + dot(current, weights(l))
            else:
                pre = dot(current, weights(l))
            s = 0.5 * jnp.tanh(0.5 * pre) + 0.5
            act = pre * s
            slopes.append(s + act * (1.0 - s))
            current = act.astype(BF16)
        store_columns(0, current)
        inputs[k][2].wait()
        save(k, 0, z_ref.at[:, span], z_hbm.at[:, span])
        save(k, 1, out_ref.at[peers, parts[0]], out_hbm.at[peers, parts[0]])
        up = columns(1).astype(F32)
        for l in range(LAYERS - 1, -1, -1):
            err = (up * slopes[l]).astype(BF16)
            err_ref[l, span, :] = err
            if l == 1:
                save(k, 2, err_ref.at[1:, span], err_hbm.at[1:, span])
            up = dot(err, weights(l), 1, 1)
        save(k, 3, err_ref.at[0, span], err_hbm.at[0, span])
        code_back = dot(err, code_matrix, 1, 1).astype(BF16)
        store_columns(1, up.astype(BF16))
        sums = dot(hot, code_back)
        pad = jnp.zeros((IMG_DEV, LANES // 2 - CODE), F32)
        for j in range(EXP_PEERS):
            low = sums[j * WIN : j * WIN + IMG_DEV]
            high = sums[j * WIN + IMG_DEV : (j + 1) * WIN]
            out_ref[k * EXP_PEERS + j, BLOCK - TAIL :, :] = jnp.concatenate([low, pad, high, pad], axis=1).astype(BF16)
        rest = slice(half_block, BLOCK)
        save(k, 4, out_ref.at[peers, rest], out_hbm.at[peers, rest])
    for store in outputs:
        store.wait()


def expert(got, window, weights):
    return pl.pallas_call(
        expert_body,
        in_specs=[in_hbm(), in_vmem(), in_vmem()],
        out_specs=[in_hbm(), in_hbm(), in_hbm(), in_vmem()],
        scratch_shapes=[
            pltpu.VMEM((PEERS, BLOCK, LANES), BF16),
            pltpu.VMEM((PEERS, BLOCK, LANES), BF16),
            pltpu.VMEM((LAYERS, SLOTS, D), BF16),
            pltpu.VMEM((LAYERS, SLOTS, D), BF16),
            pltpu.SemaphoreType.DMA((EXP_STEPS, 3)),
            pltpu.SemaphoreType.DMA((EXP_STEPS, 5)),
        ],
        out_shape=[
            pltpu.HBM((PEERS, BLOCK, LANES), BF16),
            pltpu.HBM((LAYERS, SLOTS, D), BF16),
            pltpu.HBM((LAYERS, SLOTS, D), BF16),
            jax.ShapeDtypeStruct((SLOTS, CODE), BF16),
        ],
        compiler_params=params_of(44),
        cost_estimate=cost(17),
        name="expert",
    )(*pinned(got), window, weights)


def grads_body(narrow_ref, z_ref, err_ref, code_ref, *refs):
    out_refs, (scr, order) = refs[:NARROW], refs[NARROW:]
    l = pl.program_id(0)
    scr[pl.ds(pl.multiple_of(l * D, D), D), :] = dot(z_ref[0], err_ref[0], 0, 0)

    @pl.when(l == 0)
    def _():
        scr[LAYERS * D :, :] = dot(code_ref[...], err_ref[0], 0, 0)

    @pl.when(l == LAYERS - 1)
    def _():
        for n in range(NARROW):
            order[n, :SHARD, :] = scr[n * SHARD : (n + 1) * SHARD, :].astype(BF16)
            order[n, SHARD:, :] = jnp.zeros((SHARD_PAD - SHARD, D), BF16)
        for k, ref in enumerate(out_refs):
            ref[...] = order[(narrow_ref[0] + k) % NARROW]


def grads(narrow, z, err, code):
    rows = PEERS * CAP
    return pl.pallas_call(
        grads_body,
        grid_spec=pltpu.PrefetchScalarGridSpec(
            num_scalar_prefetch=1,
            grid=(LAYERS,),
            in_specs=[
                pl.BlockSpec((1, rows, D), lambda i, n: (i, 0, 0)),
                pl.BlockSpec((1, rows, D), lambda i, n: (i, 0, 0)),
                pl.BlockSpec((rows, CODE), lambda i, n: (0, 0)),
            ],
            out_specs=[pl.BlockSpec((SHARD_PAD, D), lambda i, n: (0, 0))] * NARROW,
            scratch_shapes=[pltpu.VMEM((PROWS, D), F32), pltpu.VMEM((NARROW, SHARD_PAD, D), BF16)],
        ),
        out_shape=[jax.ShapeDtypeStruct((SHARD_PAD, D), BF16)] * NARROW,
        compiler_params=params_of(40),
        cost_estimate=cost(10),
        name="grads",
    )(narrow, z, err, code)


TILE = 8
UNROLL = 32
UNPACK_PEERS = 4
UNPACK_ROWS = 256


def unpack_body(pos_ref, back_hbm, out_hbm, feat_hbm, back_ref, slots, rows, out_ref, feat_ref, loads, sems):
    all_peers = [slice(k, k + UNPACK_PEERS) for k in range(0, PEERS, UNPACK_PEERS)]
    inputs = [pltpu.make_async_copy(back_hbm.at[p], back_ref.at[p], loads.at[k]) for k, p in enumerate(all_peers)]
    for load in inputs:
        load.start()
    n = UNPACK_PEERS * CAP
    for k, peers in enumerate(all_peers):
        inputs[k].wait()
        for half in range(2):
            for c in range(CHUNKS):
                got = back_ref[peers, column_of(half, c), :].reshape(n, LANES).astype(F32)
                slots[pl.ds(k * n * TILE + half * CHUNKS + c, n, stride=TILE), :] = got
    stores = []
    for part in range(ROWS_DEV // UNPACK_ROWS):
        span = slice(part * UNPACK_ROWS, (part + 1) * UNPACK_ROWS)

        def move(i, _):
            for u in range(UNROLL):
                r = part * UNPACK_ROWS + i * UNROLL + u
                p = pos_ref[0, r]
                rows[pl.ds(pl.multiple_of(r * TILE, TILE), TILE), :] = slots[
                    pl.ds(pl.multiple_of(p * TILE, TILE), TILE), :
                ]
            return 0

        lax.fori_loop(0, UNPACK_ROWS // UNROLL, move, 0)
        for half, (dst, hbm) in enumerate(((out_ref, out_hbm), (feat_ref, feat_hbm))):
            for c in range(CHUNKS):
                dst[span, c * LANES : (c + 1) * LANES] = rows[
                    pl.ds(part * UNPACK_ROWS * TILE + half * CHUNKS + c, UNPACK_ROWS, stride=TILE), :
                ].astype(BF16)
            store = pltpu.make_async_copy(dst.at[span], hbm.at[span], sems.at[part, half])
            store.start()
            stores.append(store)
    for store in stores:
        store.wait()


def unpack(pos, back):
    return pl.pallas_call(
        unpack_body,
        in_specs=[in_smem(), in_hbm()],
        out_specs=[in_hbm()] * 2,
        scratch_shapes=[
            pltpu.VMEM((PEERS, BLOCK, LANES), BF16),
            pltpu.VMEM((SLOTS * TILE, LANES), F32),
            pltpu.VMEM((ROWS_DEV * TILE, LANES), F32),
            pltpu.VMEM((ROWS_DEV, D), BF16),
            pltpu.VMEM((ROWS_DEV, D), BF16),
            pltpu.SemaphoreType.DMA((PEERS // UNPACK_PEERS,)),
            pltpu.SemaphoreType.DMA((ROWS_DEV // UNPACK_ROWS, 2)),
        ],
        out_shape=[pltpu.HBM((ROWS_DEV, D), BF16)] * 2,
        compiler_params=params_of(32),
        cost_estimate=cost(7),
        name="unpack",
    )(pos, *pinned(back))


def exchange(values):
    return lax.all_to_all(values, "expert", split_axis=0, concat_axis=0, tiled=True)


def shifted(block, axis, distance):
    devices = range(lax.axis_size(axis))
    route = [((i - distance) % len(devices), i) for i in devices]
    return lax.ppermute(block, axis, route)


def ring_gather(own):
    got = [own]
    ahead = behind = own
    for step in range(1, NARROW // 2 + 1):
        ahead = shifted(ahead, "narrow", 1)
        got.append(ahead)
        if step < NARROW // 2:
            behind = shifted(behind, "narrow", -1)
            got.append(behind)
    return got


def ring_reduce(terms):
    add = lambda a, b: a.astype(F32) + b.astype(F32)
    half = NARROW // 2
    ahead, behind = terms[half], terms[half + 1]
    for step in range(half):
        ahead = shifted(ahead, "narrow", 1)
        if step > 0:
            behind = shifted(behind, "narrow", -1)
        if step < half - 1:
            ahead = add(ahead, terms[half - 1 - step]).astype(BF16)
            if step > 0:
                behind = add(behind, terms[half + 1 + step]).astype(BF16)
    return finish(ahead, behind, terms[0])


def finish_body(a_ref, b_ref, c_ref, out_ref):
    total = a_ref[...].astype(F32) + b_ref[...].astype(F32) + c_ref[...].astype(F32)
    out_ref[:, 0, :] = total[:SHARD]


def finish(a, b, c):
    return pl.pallas_call(
        finish_body,
        in_specs=[in_vmem()] * 3,
        out_specs=in_vmem(),
        out_shape=jax.ShapeDtypeStruct((SHARD, 1, D), F32),
        compiler_params=params_of(8),
        cost_estimate=cost(2),
        name="finish",
    )(a, b, c)


def body(feats, cotangent, routes, image_ids, codes, params):
    flat = lax.axis_index(("expert", "narrow"))
    first_image = (flat * IMG_DEV).astype(jnp.int32).reshape(1)
    narrow = lax.axis_index("narrow").astype(jnp.int32)
    packed, pos = pack(
        first_image, routes.reshape(1, ROWS_DEV), image_ids.reshape(1, ROWS_DEV), feats, cotangent
    )
    got = exchange(packed)
    shards = ring_gather(jnp.pad(params[0], ((0, SHARD_PAD - SHARD), (0, 0))))
    weights = join(narrow.reshape(1), shards)
    ring = jnp.concatenate([codes, codes[:CAP]], axis=0)
    window = lax.dynamic_slice(ring, (narrow * IMG_DEV, 0), (PEERS * CAP, CODE))
    window = window.reshape(PEERS, CAP, CODE)[:, :WIN].reshape(PEERS * WIN, CODE)
    reply, z, err, code_rows = expert(got, window, weights)
    back = exchange(reply)
    mine = ring_reduce(grads(narrow.reshape(1), z, err, code_rows))
    back, mine = lax.optimization_barrier((back, mine))
    param_grad = mine.transpose(1, 0, 2)
    sums = jnp.sum(back[:, BLOCK - TAIL :, :].astype(F32), axis=0)
    high = shifted(sums[:, LANES // 2 : LANES // 2 + CODE], ("expert", "narrow"), 1)
    out_rows, feat_grad = unpack(pos, back)
    return (out_rows, feat_grad, param_grad, sums[:, :CODE] + high)


def solution(mesh):
    rows = P(("expert", "narrow"), None)
    in_specs = (rows, rows, rows, P(("expert", "narrow")), P(), P("expert", "narrow", None))
    out_specs = (rows, rows, P("expert", "narrow", None), rows)
    return jax.shard_map(body, mesh=mesh, in_specs=in_specs, out_specs=out_specs, check_vma=False)
```

```python
import jax
import jax.numpy as jnp
from jax import lax
from jax.experimental import pallas as pl
from jax.experimental.pallas import tpu as pltpu
from jax.sharding import PartitionSpec as P

LAYERS = 4
D = 512
CODE = 48
ROWS_DEV = 1024
IMG_DEV = 8
CAP = 64
PEERS = 32
NARROW = 8
LANES = 128
CHUNKS = D // LANES
TAIL = 8
BLOCK = 2 * CHUNKS * CAP + TAIL
SHARD = 262
SHARD_PAD = 264
PROWS = 2096
F32 = jnp.float32
BF16 = jnp.bfloat16
MIB = 1024 * 1024


def params_of(mib):
    return pltpu.CompilerParams(vmem_limit_bytes=mib * MIB)


def cost(us):
    return pl.CostEstimate(flops=0, transcendentals=0, bytes_accessed=us * 3_000_000)


def in_vmem():
    return pl.BlockSpec(memory_space=pltpu.VMEM)


def in_smem():
    return pl.BlockSpec(memory_space=pltpu.SMEM)


def in_hbm():
    return pl.BlockSpec(memory_space=pltpu.HBM)


def pinned(*values):
    return [pltpu.with_memory_space_constraint(v, pltpu.HBM) for v in values]


def dot(a, b, ca=1, cb=0):
    return lax.dot_general(a, b, (((ca,), (cb,)), ((), ())), preferred_element_type=F32)


SLOTS = PEERS * CAP
PACK_PEERS = 4


def column_of(half, c):
    r = (half * CHUNKS + c) * CAP
    return slice(r, r + CAP)


def pack_body(
    first_ref, routes_hbm, ids_hbm, feats_hbm, cot_hbm, out_hbm, pos_ref, routes_ref, ids_ref, feats_ref, cot_ref, out_ref, sems
):
    sources = (feats_ref, cot_ref)
    small, loads = [
        [pltpu.make_async_copy(hbm, ref, sems.at[i]) for i, hbm, ref in group]
        for group in (
            ((0, routes_hbm, routes_ref), (1, ids_hbm, ids_ref)),
            ((2, feats_hbm, feats_ref), (3, cot_hbm, cot_ref)),
        )
    ]
    for load in small + loads:
        load.start()
    for load in small:
        load.wait()
    width = 256
    upper = (
        lax.broadcasted_iota(jnp.int32, (width, width), 0)
        <= lax.broadcasted_iota(jnp.int32, (width, width), 1)
    ).astype(F32).astype(BF16)
    expert = lax.broadcasted_iota(jnp.int32, (PEERS, width), 0)
    base = (expert * CAP - 1).astype(F32)
    carry = jnp.zeros((PEERS, 1), F32)
    tail = jnp.zeros((PEERS, CAP), F32)
    off = ids_ref[...] - first_ref[0]
    off = (jnp.where(off < 0, off + PEERS * NARROW * IMG_DEV, off) + 1).astype(F32)
    for b in range(ROWS_DEV // width):
        part = slice(b * width, (b + 1) * width)
        hot = (routes_ref[:, part] == expert).astype(F32)
        rank = dot(hot.astype(BF16), upper) + carry
        carry = carry + jnp.sum(hot, axis=1, keepdims=True)
        pos_ref[:, part] = jnp.sum(hot * (rank + base), axis=0, keepdims=True).astype(jnp.int32)
        slot = jnp.sum(hot * rank, axis=0, keepdims=True).astype(jnp.int32) - 1
        at = (lax.broadcasted_iota(jnp.int32, (CAP, width), 0) == slot).astype(F32).astype(BF16)
        tail = tail + dot((hot * off[:, part]).astype(BF16), at, 1, 1)
    tail = jnp.concatenate([tail, jnp.zeros((PEERS, LANES - CAP), F32)], axis=1)
    n = PACK_PEERS * CAP
    stores = []
    for g in range(PEERS // PACK_PEERS):
        peers = slice(g * PACK_PEERS, (g + 1) * PACK_PEERS)
        slot = lax.broadcasted_iota(jnp.int32, (n, ROWS_DEV), 0) + g * n
        pick = (pos_ref[...] == slot).astype(F32).astype(BF16)
        for half, src in enumerate(sources):
            if g == 0:
                loads[half].wait()
            got = dot(pick, src[...]).astype(BF16)
            for c in range(CHUNKS):
                out_ref[peers, column_of(half, c), :] = got[:, c * LANES : (c + 1) * LANES].reshape(
                    PACK_PEERS, CAP, LANES
                )
        for e in range(g * PACK_PEERS, (g + 1) * PACK_PEERS):
            out_ref[e, BLOCK - TAIL :, :] = jnp.broadcast_to(tail[e : e + 1], (TAIL, LANES)).astype(BF16)
        stores.append(pltpu.make_async_copy(out_ref.at[peers], out_hbm.at[peers], sems.at[4 + g]))
        stores[-1].start()
    for store in stores:
        store.wait()


def pack(first, routes, ids, feats, cot):
    return pl.pallas_call(
        pack_body,
        in_specs=[in_smem()] + [in_hbm()] * 4,
        out_specs=[in_hbm(), in_vmem()],
        scratch_shapes=[
            pltpu.VMEM((1, ROWS_DEV), jnp.int32),
            pltpu.VMEM((1, ROWS_DEV), jnp.int32),
            pltpu.VMEM((ROWS_DEV, D), BF16),
            pltpu.VMEM((ROWS_DEV, D), BF16),
            pltpu.VMEM((PEERS, BLOCK, LANES), BF16),
            pltpu.SemaphoreType.DMA((4 + PEERS // PACK_PEERS,)),
        ],
        out_shape=[
            pltpu.HBM((PEERS, BLOCK, LANES), BF16),
            jax.ShapeDtypeStruct((1, ROWS_DEV), jnp.int32),
        ],
        compiler_params=params_of(32),
        cost_estimate=cost(8),
        name="pack",
    )(first, *pinned(routes, ids, feats, cot))


HOPS = (0, -1, 1, -2, 2, -3, 3, -4)


def join_body(narrow_ref, *refs):
    shard_refs, (out_ref, order, scr) = refs[:NARROW], refs[NARROW:]
    for hop, ref in zip(HOPS, shard_refs):
        order[(narrow_ref[0] + hop + NARROW) % NARROW] = ref[...]
    for n in range(NARROW):
        scr[n * SHARD : (n + 1) * SHARD, :] = order[n, :SHARD, :].astype(F32)
    out_ref[...] = scr[...].astype(BF16)


def join(narrow, shards):
    return pl.pallas_call(
        join_body,
        in_specs=[in_smem()] + [in_vmem()] * NARROW,
        out_specs=in_vmem(),
        scratch_shapes=[pltpu.VMEM((NARROW, SHARD_PAD, D), BF16), pltpu.VMEM((PROWS, D), F32)],
        out_shape=jax.ShapeDtypeStruct((PROWS, D), BF16),
        compiler_params=params_of(12),
        cost_estimate=cost(4),
        name="join",
    )(narrow, *shards)


EXP_PEERS = 16
EXP_ROWS = EXP_PEERS * CAP
EXP_STEPS = PEERS // EXP_PEERS
WIN = 2 * IMG_DEV


def expert_body(
    got_hbm, win_ref, w_ref, out_hbm, z_hbm, err_hbm, code_ref, got_ref, out_ref, z_ref, err_ref, loads, stores
):
    weights = lambda l: w_ref[l * D : (l + 1) * D, :]
    code_matrix = w_ref[LAYERS * D :, :]
    all_peers = [slice(k * EXP_PEERS, (k + 1) * EXP_PEERS) for k in range(EXP_STEPS)]
    half_block = CHUNKS * CAP
    parts = (slice(0, half_block), slice(2 * half_block, BLOCK), slice(half_block, 2 * half_block))
    inputs = [
        [
            pltpu.make_async_copy(got_hbm.at[peers, part], got_ref.at[peers, part], loads.at[k, i])
            for i, part in enumerate(parts)
        ]
        for k, peers in enumerate(all_peers)
    ]
    for group in inputs:
        for load in group:
            load.start()
    outputs = []

    def save(k, i, src, dst):
        outputs.append(pltpu.make_async_copy(src, dst, stores.at[k, i]))
        outputs[-1].start()

    for k, peers in enumerate(all_peers):
        span = slice(k * EXP_ROWS, (k + 1) * EXP_ROWS)

        def columns(half):
            cols = [got_ref[peers, column_of(half, c), :].reshape(EXP_ROWS, LANES) for c in range(CHUNKS)]
            return jnp.concatenate(cols, axis=1)

        def store_columns(half, value):
            for c in range(CHUNKS):
                out_ref[peers, column_of(half, c), :] = value[:, c * LANES : (c + 1) * LANES].reshape(
                    EXP_PEERS, CAP, LANES
                )

        inputs[k][0].wait()
        inputs[k][1].wait()
        image = lax.broadcasted_iota(jnp.int32, (EXP_PEERS * WIN, EXP_ROWS), 0) + 1
        key = jnp.concatenate(
            [
                jnp.where(v > 0.0, v + float(j * WIN), 0.0)
                for j in range(EXP_PEERS)
                for v in [got_ref[k * EXP_PEERS + j, BLOCK - TAIL :, :CAP].astype(F32)]
            ],
            axis=1,
        )[0:1]
        hot = (key.astype(jnp.int32) == image).astype(F32).astype(BF16)
        window = win_ref[k * EXP_PEERS * WIN : (k + 1) * EXP_PEERS * WIN, :]
        code_rows = dot(hot, window, 0, 0).astype(BF16)
        code_ref[span, :] = code_rows
        current = columns(0)
        slopes = []
        for l in range(LAYERS):
            z_ref[l, span, :] = current
            if l == 0:
                pre = dot(code_rows, code_matrix) + dot(current, weights(l))
            else:
                pre = dot(current, weights(l))
            s = 0.5 * jnp.tanh(0.5 * pre) + 0.5
            act = pre * s
            slopes.append(s + act * (1.0 - s))
            current = act.astype(BF16)
        store_columns(0, current)
        inputs[k][2].wait()
        save(k, 0, z_ref.at[:, span], z_hbm.at[:, span])
        save(k, 1, out_ref.at[peers, parts[0]], out_hbm.at[peers, parts[0]])
        up = columns(1).astype(F32)
        for l in range(LAYERS - 1, -1, -1):
            err = (up * slopes[l]).astype(BF16)
            err_ref[l, span, :] = err
            if l == 1:
                save(k, 2, err_ref.at[1:, span], err_hbm.at[1:, span])
            up = dot(err, weights(l), 1, 1)
        save(k, 3, err_ref.at[0, span], err_hbm.at[0, span])
        code_back = dot(err, code_matrix, 1, 1).astype(BF16)
        store_columns(1, up.astype(BF16))
        sums = dot(hot, code_back)
        pad = jnp.zeros((IMG_DEV, LANES // 2 - CODE), F32)
        for j in range(EXP_PEERS):
            low = sums[j * WIN : j * WIN + IMG_DEV]
            high = sums[j * WIN + IMG_DEV : (j + 1) * WIN]
            out_ref[k * EXP_PEERS + j, BLOCK - TAIL :, :] = jnp.concatenate([low, pad, high, pad], axis=1).astype(BF16)
        rest = slice(half_block, BLOCK)
        save(k, 4, out_ref.at[peers, rest], out_hbm.at[peers, rest])
    for store in outputs:
        store.wait()


def expert(got, window, weights):
    return pl.pallas_call(
        expert_body,
        in_specs=[in_hbm(), in_vmem(), in_vmem()],
        out_specs=[in_hbm(), in_hbm(), in_hbm(), in_vmem()],
        scratch_shapes=[
            pltpu.VMEM((PEERS, BLOCK, LANES), BF16),
            pltpu.VMEM((PEERS, BLOCK, LANES), BF16),
            pltpu.VMEM((LAYERS, SLOTS, D), BF16),
            pltpu.VMEM((LAYERS, SLOTS, D), BF16),
            pltpu.SemaphoreType.DMA((EXP_STEPS, 3)),
            pltpu.SemaphoreType.DMA((EXP_STEPS, 5)),
        ],
        out_shape=[
            pltpu.HBM((PEERS, BLOCK, LANES), BF16),
            pltpu.HBM((LAYERS, SLOTS, D), BF16),
            pltpu.HBM((LAYERS, SLOTS, D), BF16),
            jax.ShapeDtypeStruct((SLOTS, CODE), BF16),
        ],
        compiler_params=params_of(44),
        cost_estimate=cost(17),
        name="expert",
    )(*pinned(got), window, weights)


def grads_body(narrow_ref, z_ref, err_ref, code_ref, *refs):
    out_refs, (scr, order) = refs[:NARROW], refs[NARROW:]
    l = pl.program_id(0)
    scr[pl.ds(pl.multiple_of(l * D, D), D), :] = dot(z_ref[0], err_ref[0], 0, 0)

    @pl.when(l == 0)
    def _():
        scr[LAYERS * D :, :] = dot(code_ref[...], err_ref[0], 0, 0)

    @pl.when(l == LAYERS - 1)
    def _():
        for n in range(NARROW):
            order[n, :SHARD, :] = scr[n * SHARD : (n + 1) * SHARD, :].astype(BF16)
            order[n, SHARD:, :] = jnp.zeros((SHARD_PAD - SHARD, D), BF16)
        for k, ref in enumerate(out_refs):
            ref[...] = order[(narrow_ref[0] + k) % NARROW]


def grads(narrow, z, err, code):
    rows = PEERS * CAP
    return pl.pallas_call(
        grads_body,
        grid_spec=pltpu.PrefetchScalarGridSpec(
            num_scalar_prefetch=1,
            grid=(LAYERS,),
            in_specs=[
                pl.BlockSpec((1, rows, D), lambda i, n: (i, 0, 0)),
                pl.BlockSpec((1, rows, D), lambda i, n: (i, 0, 0)),
                pl.BlockSpec((rows, CODE), lambda i, n: (0, 0)),
            ],
            out_specs=[pl.BlockSpec((SHARD_PAD, D), lambda i, n: (0, 0))] * NARROW,
            scratch_shapes=[pltpu.VMEM((PROWS, D), F32), pltpu.VMEM((NARROW, SHARD_PAD, D), BF16)],
        ),
        out_shape=[jax.ShapeDtypeStruct((SHARD_PAD, D), BF16)] * NARROW,
        compiler_params=params_of(40),
        cost_estimate=cost(10),
        name="grads",
    )(narrow, z, err, code)


TILE = 8
UNROLL = 32
UNPACK_PEERS = 4
UNPACK_ROWS = 256


def unpack_body(pos_ref, back_hbm, out_hbm, feat_hbm, back_ref, slots, rows, out_ref, feat_ref, loads, sems):
    all_peers = [slice(k, k + UNPACK_PEERS) for k in range(0, PEERS, UNPACK_PEERS)]
    inputs = [pltpu.make_async_copy(back_hbm.at[p], back_ref.at[p], loads.at[k]) for k, p in enumerate(all_peers)]
    for load in inputs:
        load.start()
    n = UNPACK_PEERS * CAP
    for k, peers in enumerate(all_peers):
        inputs[k].wait()
        for half in range(2):
            for c in range(CHUNKS):
                got = back_ref[peers, column_of(half, c), :].reshape(n, LANES).astype(F32)
                slots[pl.ds(k * n * TILE + half * CHUNKS + c, n, stride=TILE), :] = got
    stores = []
    for part in range(ROWS_DEV // UNPACK_ROWS):
        span = slice(part * UNPACK_ROWS, (part + 1) * UNPACK_ROWS)

        def move(i, _):
            for u in range(UNROLL):
                r = part * UNPACK_ROWS + i * UNROLL + u
                p = pos_ref[0, r]
                rows[pl.ds(pl.multiple_of(r * TILE, TILE), TILE), :] = slots[
                    pl.ds(pl.multiple_of(p * TILE, TILE), TILE), :
                ]
            return 0

        lax.fori_loop(0, UNPACK_ROWS // UNROLL, move, 0)
        for half, (dst, hbm) in enumerate(((out_ref, out_hbm), (feat_ref, feat_hbm))):
            for c in range(CHUNKS):
                dst[span, c * LANES : (c + 1) * LANES] = rows[
                    pl.ds(part * UNPACK_ROWS * TILE + half * CHUNKS + c, UNPACK_ROWS, stride=TILE), :
                ].astype(BF16)
            store = pltpu.make_async_copy(dst.at[span], hbm.at[span], sems.at[part, half])
            store.start()
            stores.append(store)
    for store in stores:
        store.wait()


def unpack(pos, back):
    return pl.pallas_call(
        unpack_body,
        in_specs=[in_smem(), in_hbm()],
        out_specs=[in_hbm()] * 2,
        scratch_shapes=[
            pltpu.VMEM((PEERS, BLOCK, LANES), BF16),
            pltpu.VMEM((SLOTS * TILE, LANES), F32),
            pltpu.VMEM((ROWS_DEV * TILE, LANES), F32),
            pltpu.VMEM((ROWS_DEV, D), BF16),
            pltpu.VMEM((ROWS_DEV, D), BF16),
            pltpu.SemaphoreType.DMA((PEERS // UNPACK_PEERS,)),
            pltpu.SemaphoreType.DMA((ROWS_DEV // UNPACK_ROWS, 2)),
        ],
        out_shape=[pltpu.HBM((ROWS_DEV, D), BF16)] * 2,
        compiler_params=params_of(32),
        cost_estimate=cost(7),
        name="unpack",
    )(pos, *pinned(back))


def exchange(values):
    return lax.all_to_all(values, "expert", split_axis=0, concat_axis=0, tiled=True)


def shifted(block, axis, distance):
    devices = range(lax.axis_size(axis))
    route = [((i - distance) % len(devices), i) for i in devices]
    return lax.ppermute(block, axis, route)


def ring_gather(own):
    got = [own]
    ahead = behind = own
    for step in range(1, NARROW // 2 + 1):
        ahead = shifted(ahead, "narrow", 1)
        got.append(ahead)
        if step < NARROW // 2:
            behind = shifted(behind, "narrow", -1)
            got.append(behind)
    return got


def ring_reduce(terms):
    add = lambda a, b: a.astype(F32) + b.astype(F32)
    half = NARROW // 2
    ahead, behind = terms[half], terms[half + 1]
    for step in range(half):
        ahead = shifted(ahead, "narrow", 1)
        if step > 0:
            behind = shifted(behind, "narrow", -1)
        if step < half - 1:
            ahead = add(ahead, terms[half - 1 - step]).astype(BF16)
            if step > 0:
                behind = add(behind, terms[half + 1 + step]).astype(BF16)
    return finish(ahead, behind, terms[0])


def finish_body(a_ref, b_ref, c_ref, out_ref):
    total = a_ref[...].astype(F32) + b_ref[...].astype(F32) + c_ref[...].astype(F32)
    out_ref[:, 0, :] = total[:SHARD]


def finish(a, b, c):
    return pl.pallas_call(
        finish_body,
        in_specs=[in_vmem()] * 3,
        out_specs=in_vmem(),
        out_shape=jax.ShapeDtypeStruct((SHARD, 1, D), F32),
        compiler_params=params_of(8),
        cost_estimate=cost(2),
        name="finish",
    )(a, b, c)


def body(feats, cotangent, routes, image_ids, codes, params):
    flat = lax.axis_index(("expert", "narrow"))
    first_image = (flat * IMG_DEV).astype(jnp.int32).reshape(1)
    narrow = lax.axis_index("narrow").astype(jnp.int32)
    packed, pos = pack(
        first_image, routes.reshape(1, ROWS_DEV), image_ids.reshape(1, ROWS_DEV), feats, cotangent
    )
    got = exchange(packed)
    shards = ring_gather(jnp.pad(params[0], ((0, SHARD_PAD - SHARD), (0, 0))))
    weights = join(narrow.reshape(1), shards)
    ring = jnp.concatenate([codes, codes[:CAP]], axis=0)
    window = lax.dynamic_slice(ring, (narrow * IMG_DEV, 0), (PEERS * CAP, CODE))
    window = window.reshape(PEERS, CAP, CODE)[:, :WIN].reshape(PEERS * WIN, CODE)
    reply, z, err, code_rows = expert(got, window, weights)
    back = exchange(reply)
    mine = ring_reduce(grads(narrow.reshape(1), z, err, code_rows))
    back, mine = lax.optimization_barrier((back, mine))
    param_grad = mine.transpose(1, 0, 2)
    sums = jnp.sum(back[:, BLOCK - TAIL :, :].astype(F32), axis=0)
    out_rows, feat_grad = unpack(pos, back)
    out_rows, feat_grad, sums = lax.optimization_barrier((out_rows, feat_grad, sums))
    high = shifted(sums[:, LANES // 2 : LANES // 2 + CODE], ("expert", "narrow"), 1)
    return (out_rows, feat_grad, param_grad, sums[:, :CODE] + high)


def solution(mesh):
    rows = P(("expert", "narrow"), None)
    in_specs = (rows, rows, rows, P(("expert", "narrow")), P(), P("expert", "narrow", None))
    out_specs = (rows, rows, P("expert", "narrow", None), rows)
    return jax.shard_map(body, mesh=mesh, in_specs=in_specs, out_specs=out_specs, check_vma=False)
```
